512 devices in a mesh: blk: 32 (over x_hi, z, core), pair: 16 (over y, x_lo).
Axes of the slice: x: 4 (x_hi: 2, x_lo: 2; x = x_hi * 2 + x_lo), y: 8, z: 8, core: 2. Of those that a mesh axis runs over, the one named last changes fastest.
Arguments:
- first_feat: bfloat16 [32, 30720, 128], P('pair', 'blk'), parts along dimension 0, may hold values from -8 to 8
- second_feat: bfloat16 [32, 30720, 128], P('pair', 'blk'), parts along dimension 0, may hold values from -8 to 8
- conv_weight: float32 [4, 4, 3, 3], replicated, may hold values from -1 to 1
- conv_bias: float32 [4], replicated, may hold values from -0.5 to 0.5
Outputs:
- refined: float32 [32, 4, 64, 480], P('pair', None, 'blk'), parts along dimension 0
The draws below stay inside these ranges and needn't reach their ends.
There are 16 independent parts, one for each index of `pair`. The reference program is written for one: setup_inputs(seed, part) draws one part's arguments, and reference() takes and returns one part's arrays. A program takes and returns all parts, laid end to end along the dimension named above; an argument that names none is the same for every part. Nothing has to cross between parts.
All inputs are finite; a program needn't handle non-finite values.
Results may differ from the reference program's by a relative error of at most 0.0003.
Values may be sent and summed in bfloat16 or wider, within the bound.
No kernel may reach another device: no remote copies, remote signals or barrier semaphores. Data moves between devices by JAX's collectives and lax.ppermute only.
A program may use at most 128 MiB of HBM per device.

```python
import math
import jax
import jax.numpy as jnp
from jax import lax

C = 128
W = 480
ROWS_DEV = 2
FRAMES = 2
H = 64
N_BLK = 32


def source_order(key):
    pixels = H * W
    position = jnp.arange(pixels, dtype=jnp.int32)
    row_index = position // W
    parity = position % W % 2
    group = (row_index + parity * (ROWS_DEV // 2)) // ROWS_DEV * 2 + parity
    noise_rank = jax.random.randint(key, (pixels,), 0, 1048576, dtype=jnp.int32)
    by_position = jnp.argsort(group, stable=True)
    by_random = jnp.argsort(group * 1048576 + noise_rank, stable=True)
    return jnp.zeros((pixels,), jnp.int32).at[by_position].set(by_random.astype(jnp.int32))


def drawn_pair(key):
    base = jax.random.fold_in(key, 211)
    keys = jax.random.split(base, 5)
    pixels = H * W
    source = source_order(keys[0])
    first = jnp.clip(jax.random.normal(keys[1], (pixels, C), jnp.float32), -6.0, 6.0)
    second = first[source] + 0.5 * jnp.clip(jax.random.normal(keys[4], (pixels, C), jnp.float32), -6.0, 6.0)
    return (jnp.clip(first, -7.9, 7.9), jnp.clip(second, -7.9, 7.9))


def all_pairs(key):
    firsts = []
    seconds = []
    for frame in range(FRAMES):
        first, second = drawn_pair(jax.random.fold_in(key, 1000 + frame))
        firsts.append(first)
        seconds.append(second)
    return (jnp.stack(firsts), jnp.stack(seconds))


def draw_first_feat(key, part):
    return all_pairs(key)[0].astype(jnp.bfloat16)


def draw_second_feat(key, part):
    return all_pairs(key)[1].astype(jnp.bfloat16)


def gaussian(own_key, shape, deviation, reach, kind=jnp.bfloat16):
    values = jax.random.normal(own_key, shape, jnp.float32) * deviation
    return jnp.minimum(jnp.maximum(values, -reach), reach).astype(kind)


def setup_inputs(seed: int = 0, part: int = 0) -> dict:
    seeds = jax.random.split(jax.random.key(seed), 5)
    part_keys = jax.random.split(jax.random.fold_in(seeds[4], part), 5)
    return {
        "first_feat": draw_first_feat(jax.random.fold_in(jax.random.fold_in(seeds[4], part), 71), part),
        "second_feat": draw_second_feat(jax.random.fold_in(jax.random.fold_in(seeds[4], part), 71), part),
        "conv_weight": gaussian(seeds[2], (4, 4, 3, 3), 0.25, 1.0, jnp.float32),
        "conv_bias": jnp.clip(jax.random.uniform(seeds[3], (4,), jnp.float32, -0.5, 0.5), -0.5, 0.5),
    }


def coordinates(position):
    row_index = (position // W).astype(jnp.float32)
    col_index = (position % W).astype(jnp.float32)
    return ((2.0 * col_index + 1.0) / W - 1.0, (2.0 * row_index + 1.0) / H - 1.0)

def expect_flow(queries, key_rows):
    tile_pixels = ROWS_DEV * W
    padded = jnp.pad(key_rows, ((tile_pixels, tile_pixels), (0, 0)))
    inverse_root = 1.0 / math.sqrt(C)

    def match_tile(tile):
        query_block = lax.dynamic_slice_in_dim(queries, tile * tile_pixels, tile_pixels, 0)
        key_block = lax.dynamic_slice_in_dim(padded, tile * tile_pixels, 3 * tile_pixels, 0)
        position = (tile - 1) * tile_pixels + jnp.arange(3 * tile_pixels, dtype=jnp.int32)
        inside = (position >= 0) & (position < H * W)
        key_x, key_y = coordinates(position)
        scores = jnp.dot(query_block, key_block.T, preferred_element_type=jnp.float32) * inverse_root
        scores = jnp.where(inside[None, :], scores, -jnp.inf)
        highest = lax.optimization_barrier(jnp.max(scores, axis=1, keepdims=True))
        weights = jnp.exp(scores - highest)
        totals = lax.optimization_barrier(jnp.sum(weights, axis=1))
        return (lax.optimization_barrier(jnp.sum(weights * key_x[None, :], axis=1)) / totals, lax.optimization_barrier(jnp.sum(weights * key_y[None, :], axis=1)) / totals)
    expect_x, expect_y = lax.map(match_tile, jnp.arange(N_BLK, dtype=jnp.int32))
    own_x, own_y = coordinates(jnp.arange(H * W, dtype=jnp.int32))
    return (expect_x.reshape(-1) - own_x, expect_y.reshape(-1) - own_y)

def refine_pair(first_one, second_one, conv_weight, conv_bias):
    forward_x, forward_y = expect_flow(first_one, second_one)
    backward_x, backward_y = expect_flow(second_one, first_one)
    flow = jnp.stack([forward_x, forward_y, backward_x, backward_y]).reshape(4, H, W)
    extended = jnp.pad(flow, ((0, 0), (1, 1), (1, 1)))
    mixture = jnp.zeros_like(flow)
    for row_tap in range(3):
        for col_tap in range(3):
            window = extended[:, row_tap:row_tap + H, col_tap:col_tap + W]
            mixture = mixture + jnp.einsum('oi,irc->orc', conv_weight[:, :, row_tap, col_tap], window, precision=lax.Precision.HIGHEST)
    return flow + mixture + conv_bias[:, None, None]

def reference(first_feat, second_feat, conv_weight, conv_bias):
    results = [refine_pair(first_feat[frame], second_feat[frame], conv_weight, conv_bias) for frame in range(FRAMES)]
    return jnp.stack(results)
```

```python
import functools
import math

import jax
import jax.numpy as jnp
from jax import lax
from jax.experimental import pallas as pl
from jax.experimental.pallas import tpu as pltpu
from jax.sharding import PartitionSpec as P


W = 480
TILE = 960
CH = 128
FR = 2
MID = 240.0
SCALE = math.log2(math.e) / math.sqrt(CH)
LOW = 2.0**-60
HIGH = 2.0**100
CHUNKS = ((0, 256), (256, 256), (512, 256), (768, 192))
NT = (((1,), (1,)), ((), ()))
NN = (((1,), (0,)), ((), ()))


def dot(a, b, dims):
    return lax.dot_general(a, b, dims, preferred_element_type=jnp.float32)


def side():
    pos = lax.axis_index("blk")
    even = pos % 2 == 0
    present = jnp.where(even, pos > 0, pos < lax.axis_size("blk") - 1)
    return even, present


def moments():
    lane = lax.broadcasted_iota(jnp.int32, (8, TILE), 1)
    row = lax.broadcasted_iota(jnp.int32, (8, TILE), 0)
    second = (lane >= W).astype(jnp.int32)
    col = lane - W * second - int(MID)
    value = jnp.where(row == 0, 1, jnp.where(row == 1, col, jnp.where(row == 2, second, 0)))
    return value.astype(jnp.float32).astype(jnp.bfloat16)


def split_into(dst, feat):
    scaled = feat.astype(jnp.float32) * SCALE
    hi = scaled.astype(jnp.bfloat16)
    dst[:, :CH] = hi
    dst[:, CH:] = (scaled - hi.astype(jnp.float32)).astype(jnp.bfloat16)


def twice_into(dst, feat):
    dst[:, :CH] = feat
    dst[:, CH:] = feat


def sums(lhs, rhs, mom, down, across=False):
    total = None
    for n0, w in CHUNKS:
        weight = jnp.exp2(dot(lhs[...], rhs[n0 : n0 + w, :], NT)).astype(jnp.bfloat16)
        down(n0, w, dot(mom, weight, NN))
        if across:
            part = dot(mom[:, n0 : n0 + w], weight, NT)
            total = part if total is None else total + part
    return total


def own_kernel(first, second, fwd, bwd, fs, ss):
    mom = moments()

    def frame(f, _):
        split_into(fs, first[f])
        twice_into(ss, second[f])

        def down(n0, w, part):
            fwd[f, :, n0 : n0 + w] = part

        bwd[f] = sums(ss, fs, mom, down, across=True)
        return 0

    lax.fori_loop(0, FR, frame, 0)


def shift_y(part, offset):
    row = lax.broadcasted_iota(jnp.int32, part.shape, 0)
    return part + jnp.where(row == 2, offset * part[0:1, :], 0.0)


def chip_kernel(first, second, first_p, second_p, fwd0, bwd0, fwd, bwd, fs, ss, fp, sp):
    mom = moments()
    even, _ = side()
    offset = jnp.where(even, 2.0, -2.0)

    def frame(f, _):
        split_into(fs, first[f])
        twice_into(ss, second[f])
        split_into(fp, first_p[f])
        twice_into(sp, second_p[f])

        def down_f(n0, w, part):
            fwd[f, :, n0 : n0 + w] = fwd0[f, :, n0 : n0 + w] + shift_y(part, offset)

        def down_b(n0, w, part):
            bwd[f, :, n0 : n0 + w] = bwd0[f, :, n0 : n0 + w] + shift_y(part, offset)

        sums(sp, fs, mom, down_f)
        sums(fp, ss, mom, down_b)
        return 0

    lax.fori_loop(0, FR, frame, 0)


def merge(a, b):
    top = jnp.maximum(a[0], b[0])
    ka, kb = jnp.exp2(a[0] - top), jnp.exp2(b[0] - top)
    return (top,) + tuple(u * ka + v * kb for u, v in zip(a[1:], b[1:]))


def finish(total, mom_x, mom_y, row, height):
    col = lax.broadcasted_iota(jnp.int32, total.shape, 1).astype(jnp.float32) - MID
    return (mom_x / total - col) * (2.0 / W), (mom_y / total - row) * (2.0 / height)


def halves(x):
    return x[:, :W], x[:, W:]


def far_kernel(height, first, second, first_p, second_p, second_o, fwd0, bwd0,
               msg, loc, fs, so, fwd, col, bwd, feats, tops):
    mom = moments()
    even, present = side()
    here = jnp.where(present, 1.0, 0.0)
    far = jnp.where(even, -2.0, 2.0)
    near = -far

    def frame(f, _):
        split_into(fs, first[f])
        twice_into(so, second_o[f])

        def down(n0, w, part):
            fwd[f, :, n0 : n0 + w] = fwd0[f, :, n0 : n0 + w] + here * shift_y(part, far)

        col[f] = here * sums(so, fs, mom, down, across=True)
        bwd[f] = bwd0[f]
        return 0

    lax.fori_loop(0, FR, frame, 0)
    tops[...] = jnp.zeros_like(tops)

    def inside(x):
        return jnp.all((x >= LOW) & (x <= HIGH))

    good = inside(fwd[:, 0:1, :]) & inside(bwd[:, 0:1, :])
    good &= inside(col[:, 0:1, :]) | jnp.logical_not(present)

    @pl.when(jnp.logical_not(good))
    def _():
        index = lax.broadcasted_iota(jnp.int32, (TILE, 1), 0)
        second_row = (index >= W).astype(jnp.float32)
        column = index.astype(jnp.float32) - W * second_row - MID

        def frame(f, _):
            for k, src in enumerate((second, second_p, second_o, first, first_p)):
                feats[k] = src[f]

            def job(dst, slot, query, begin, count):
                for n0 in range(0, TILE, CH):
                    w = min(CH, TILE - n0)
                    rows = query[f, n0 : n0 + w, :]

                    def step(k, old):
                        scores = dot(feats[k], rows, NT) * SCALE
                        rel = k - begin
                        offset = jnp.where(rel == 0, 0.0, jnp.where(rel == 1, near, far))
                        use = jnp.where((rel < 2) | present, 1.0, 0.0)
                        top = jnp.max(scores, axis=0, keepdims=True)
                        weight = jnp.exp2(scores - top) * use
                        total = jnp.sum(weight, axis=0, keepdims=True)
                        fresh = (
                            jnp.where(use > 0, top, -1e30),
                            total,
                            jnp.sum(weight * column, axis=0, keepdims=True),
                            jnp.sum(weight * second_row, axis=0, keepdims=True) + offset * total,
                        )
                        return merge(old, fresh)

                    zero = jnp.zeros((1, w), jnp.float32)
                    status = (jnp.full((1, w), -1e30, jnp.float32), zero, zero, zero)
                    status = lax.fori_loop(begin, begin + count, step, status)
                    tops[f, slot : slot + 1, n0 : n0 + w] = status[0]
                    for k in range(3):
                        dst[f, k : k + 1, n0 : n0 + w] = status[1 + k]

            job(fwd, 0, first, 0, 3)
            job(bwd, 1, second, 3, 2)
            job(col, 2, second_o, 3, 1)
            return 0

        lax.fori_loop(0, FR, frame, 0)

    def pack(f, _):
        g_o = jnp.concatenate([tops[f, 2:3, :], col[f, 0:3, :]], axis=0)
        g_i = jnp.concatenate([tops[f, 1:2, :], bwd[f, 0:3, :]], axis=0)
        o0, o1 = halves(g_o)
        i0, i1 = halves(g_i)
        flows = []
        for row, stat in enumerate(halves(fwd[f, 0:3, :])):
            fx, fy = finish(stat[0:1], stat[1:2], stat[2:3], float(row), height)
            flows.append(jnp.concatenate([fx, fy], axis=0))
        blank = jnp.zeros((2, W), jnp.float32)
        msg[f, 0:4, :] = o0
        msg[f, 4:8, :] = o1
        msg[f, 8:12, :] = jnp.where(even, i0, i1)
        msg[f, 12:14, :] = jnp.where(even, flows[0], flows[1])
        msg[f, 14:16, :] = blank
        loc[f, 0:4, :] = i0
        loc[f, 4:8, :] = i1
        loc[f, 8:10, :] = flows[0]
        loc[f, 10:12, :] = flows[1]
        return 0

    lax.fori_loop(0, FR, pack, 0)


def flow_kernel(height, loc, sent, got, rows, edge):
    even, present = side()
    far = jnp.where(even, -2.0, 2.0)

    def stat(x, offset, keep=None):
        top, total, mx, my = x[0:1], x[1:2], x[2:3], x[3:4]
        if keep is not None:
            top = jnp.where(keep, top, -1e30)
        return top, total, mx, my + offset * total

    for f in range(FR):
        maps = []
        for r in range(2):
            _, total, mx, my = merge(
                stat(loc[f, 4 * r : 4 * r + 4, :], 0.0),
                stat(got[f, 4 * r : 4 * r + 4, :], far, present),
            )
            bx, by = finish(total, mx, my, float(r), height)
            maps.append(jnp.concatenate([loc[f, 8 + 2 * r : 10 + 2 * r, :], bx, by], axis=0))
        mine = jnp.where(even, sent[f, 4:8, :], sent[f, 0:4, :])
        _, total, mx, my = merge(stat(got[f, 8:12, :], 0.0, present), stat(mine, -far))
        total = jnp.where(present, total, 1.0)
        bx, by = finish(total, mx, my, jnp.where(even, 1.0, 0.0), height)
        halo = jnp.concatenate([got[f, 12:14, :], bx, by], axis=0)
        halo = jnp.where(present, halo, 0.0)
        edge[f] = jnp.where(even, maps[1], maps[0])
        rows[f, 0:4, :] = jnp.where(even, halo, 0.0)
        rows[f, 4:8, :] = maps[0]
        rows[f, 8:12, :] = maps[1]
        rows[f, 12:16, :] = jnp.where(even, 0.0, halo)


def refine_kernel(rows, edge, taps, bias, out):
    even, _ = side()
    none = jnp.zeros((16, 1), jnp.float32)
    for f in range(FR):
        mine = rows[f]
        other = edge[f]
        full = jnp.concatenate(
            [jnp.where(even, mine[0:4], other), mine[4:12], jnp.where(even, other, mine[12:16])], axis=0
        )
        left = jnp.concatenate([none, full[:, : W - 1]], axis=1)
        right = jnp.concatenate([full[:, 1:], none], axis=1)
        patches = jnp.concatenate([left, full, right], axis=0)
        mixed = lax.dot_general(
            taps[...], patches, NN, precision=lax.Precision.HIGHEST, preferred_element_type=jnp.float32
        )
        mixed = mixed + bias[...] + full[4:12]
        for o in range(4):
            out[f, o, 0:1, :] = mixed[o : o + 1]
            out[f, o, 1:2, :] = mixed[4 + o : 5 + o]


def call(kernel, shapes, scratch, limit, flops, *args):
    spec = pl.BlockSpec(memory_space=pltpu.VMEM)
    single = not isinstance(shapes, tuple)
    return pl.pallas_call(
        kernel,
        out_shape=shapes,
        in_specs=[spec] * len(args),
        out_specs=spec if single else (spec,) * len(shapes),
        scratch_shapes=scratch,
        compiler_params=pltpu.CompilerParams(vmem_limit_bytes=limit << 20),
        cost_estimate=pl.CostEstimate(flops=flops, bytes_accessed=flops // 1000, transcendentals=0),
    )(*args)


def device_program(first, second, conv_weight, conv_bias):
    size = lax.axis_size("blk")
    height = 2 * size
    f32 = functools.partial(jax.ShapeDtypeStruct, dtype=jnp.float32)
    wide = pltpu.VMEM((TILE, 2 * CH), jnp.bfloat16)
    chip = [(i, i ^ 1) for i in range(size)]
    far = [(i, i - 1 if i % 2 == 0 else i + 1) for i in range(1, size - 1)]

    second_o = lax.ppermute(second, "blk", far)
    second_p = lax.ppermute(second, "blk", chip)
    first_p = lax.ppermute(first, "blk", chip)
    stats = f32((FR, 8, TILE))
    fwd, bwd = call(own_kernel, (stats, stats), [wide] * 2, 16, 10**9, first, second)
    fwd, bwd = call(chip_kernel, (stats, stats), [wide] * 4, 16, 2 * 10**9,
                    first, second, first_p, second_p, fwd, bwd)
    kept = pltpu.VMEM((FR, 8, TILE), jnp.float32)
    msg, loc = call(functools.partial(far_kernel, height), (f32((FR, 16, W)),) * 2,
                    [wide] * 2 + [kept] * 3 + [pltpu.VMEM((5, TILE, CH), jnp.bfloat16), kept], 24, 10**9,
                    first, second, first_p, second_p, second_o, fwd, bwd)
    got = lax.ppermute(msg, "blk", far)
    rows, edge = call(functools.partial(flow_kernel, height), (f32((FR, 16, W)), f32((FR, 4, W))), [], 4, 10**6,
                      loc, msg, got)
    other = lax.ppermute(edge, "blk", chip)
    taps = conv_weight.transpose(0, 3, 2, 1)
    taps = jnp.stack([jnp.pad(taps, ((0, 0), (0, 0), (r, 1 - r), (0, 0))) for r in range(2)])
    taps = taps.reshape(8, 48)
    bias = jnp.concatenate([conv_bias, conv_bias]).reshape(8, 1)
    return call(refine_kernel, f32((FR, 4, 2, W)), [], 4, 10**6, rows, other, taps, bias)


def solution(mesh):
    placed = (P("pair", "blk", None), P("pair", "blk", None), P(), P())
    return jax.shard_map(
        device_program,
        mesh=mesh,
        in_specs=placed,
        out_specs=P("pair", None, "blk", None),
        check_vma=False,
    )
```

```python
import functools
import math

import jax
import jax.numpy as jnp
from jax import lax
from jax.experimental import pallas as pl
from jax.experimental.pallas import tpu as pltpu
from jax.sharding import PartitionSpec as P


W = 480
TILE = 960
CH = 128
FR = 2
MID = 240.0
SCALE = math.log2(math.e) / math.sqrt(CH)
LOW = 2.0**-60
HIGH = 2.0**100
NT = (((1,), (1,)), ((), ()))
NN = (((1,), (0,)), ((), ()))


def dot(a, b, dims):
    return lax.dot_general(a, b, dims, preferred_element_type=jnp.float32)


def side():
    pos = lax.axis_index("blk")
    even = pos % 2 == 0
    present = jnp.where(even, pos > 0, pos < lax.axis_size("blk") - 1)
    return even, present


def moments():
    lane = lax.broadcasted_iota(jnp.int32, (8, TILE), 1)
    row = lax.broadcasted_iota(jnp.int32, (8, TILE), 0)
    second = (lane >= W).astype(jnp.int32)
    col = lane - W * second - int(MID)
    value = jnp.where(row == 0, 1, jnp.where(row == 1, col, jnp.where(row == 2, second, 0)))
    return value.astype(jnp.float32).astype(jnp.bfloat16)


def split_into(dst, f, feat):
    scaled = feat.astype(jnp.float32) * SCALE
    hi = scaled.astype(jnp.bfloat16)
    dst[f, :, :CH] = hi
    dst[f, :, CH:] = (scaled - hi.astype(jnp.float32)).astype(jnp.bfloat16)


def twice_into(dst, f, feat):
    dst[f, :, :CH] = feat
    dst[f, :, CH:] = feat


def down_sums(weight):
    total = ramp = later = None
    for r in range(2):
        run = None
        for g in range(r * W, (r + 1) * W, 8):
            part = weight[g : g + 8]
            run = part if run is None else run + part
            ramp = run if ramp is None else ramp + run
        total = run if total is None else total + run
        later = run
    sub = lax.broadcasted_iota(jnp.int32, total.shape, 0).astype(jnp.float32)
    col = (W - MID + sub) * total - 8.0 * ramp
    rows = [jnp.sum(v, axis=0, keepdims=True) for v in (total, col, later)]
    return jnp.concatenate(rows + [jnp.zeros((5, total.shape[1]), jnp.float32)], axis=0)


def sums(lhs, rhs, f, down, mom=None):
    size = 256 if mom is None else 512
    cuts = [(n0, min(size, TILE - n0)) for n0 in range(0, TILE, size)]

    def scores(n0, w):
        return dot(lhs[f], rhs[f, n0 : n0 + w, :], NT)

    across = None
    ahead = scores(*cuts[0])
    for i, (n0, w) in enumerate(cuts):
        weight = jnp.exp2(ahead)
        if i + 1 < len(cuts):
            ahead = scores(*cuts[i + 1])
        down(n0, w, down_sums(weight))
        if mom is not None:
            part = dot(mom[:, n0 : n0 + w], weight.astype(jnp.bfloat16), NT)
            across = part if across is None else across + part
    return across


def own_block(first, second, fwd, bwd, fs, ss, fbuf, sbuf, sems):
    copies = []
    for f in range(FR):
        for k, (src, dst) in enumerate(((first, fbuf), (second, sbuf))):
            copies.append(pltpu.make_async_copy(src.at[f], dst.at[f], sems.at[2 * f + k]))
    for c in copies:
        c.start()
    mom = moments()
    for c in copies:
        c.wait()

    def frame(f, _):
        split_into(fs, f, fbuf[f])
        twice_into(ss, f, sbuf[f])

        def down(n0, w, part):
            fwd[f, :, n0 : n0 + w] = part

        bwd[f] = sums(ss, fs, f, down, mom)
        return 0

    lax.fori_loop(0, FR, frame, 0)


def even_kernel(*refs):
    even, _ = side()

    @pl.when(even)
    def _():
        own_block(*refs)


def shift_y(part, offset):
    row = lax.broadcasted_iota(jnp.int32, part.shape, 0)
    return part + jnp.where(row == 2, offset * part[0:1, :], 0.0)


def chip_kernel(first, second, first_p, second_p, fwd0, bwd0, fs0, ss0, fwd, bwd, fs, ss, fp, sp, fbuf, sbuf, sems):
    even, _ = side()
    offset = jnp.where(even, 2.0, -2.0)

    @pl.when(jnp.logical_not(even))
    def _():
        own_block(first, second, fwd, bwd, fs, ss, fbuf, sbuf, sems)

    def frame(f, _):
        split_into(fp, f, first_p[f])
        twice_into(sp, f, second_p[f])

        def down_f(n0, w, part):
            fwd[f, :, n0 : n0 + w] += shift_y(part, offset)

        def down_b(n0, w, part):
            bwd[f, :, n0 : n0 + w] += shift_y(part, offset)

        sums(sp, fs, f, down_f)
        sums(fp, ss, f, down_b)
        return 0

    lax.fori_loop(0, FR, frame, 0)


def merge(a, b):
    top = jnp.maximum(a[0], b[0])
    ka, kb = jnp.exp2(a[0] - top), jnp.exp2(b[0] - top)
    return (top,) + tuple(u * ka + v * kb for u, v in zip(a[1:], b[1:]))


def finish(total, mom_x, mom_y, row, height):
    col = lax.broadcasted_iota(jnp.int32, total.shape, 1).astype(jnp.float32) - MID
    return (mom_x / total - col) * (2.0 / W), (mom_y / total - row) * (2.0 / height)


def halves(x):
    return x[:, :W], x[:, W:]


def far_kernel(height, first, second, first_p, second_p, second_o, fwd0, bwd0, fs,
               msg, loc, so, fwd, col, bwd, feats, tops, sems):
    mom = moments()
    even, present = side()
    here = jnp.where(present, 1.0, 0.0)
    far = jnp.where(even, -2.0, 2.0)
    near = -far

    def frame(f, _):
        twice_into(so, f, second_o[f])

        def down(n0, w, part):
            fwd[f, :, n0 : n0 + w] = fwd0[f, :, n0 : n0 + w] + here * shift_y(part, far)

        col[f] = here * sums(so, fs, f, down, mom)
        bwd[f] = bwd0[f]
        return 0

    lax.fori_loop(0, FR, frame, 0)
    tops[...] = jnp.zeros_like(tops)

    def inside(x):
        return jnp.all((x >= LOW) & (x <= HIGH))

    good = inside(fwd[:, 0:1, :]) & inside(bwd[:, 0:1, :])
    good &= inside(col[:, 0:1, :]) | jnp.logical_not(present)

    @pl.when(jnp.logical_not(good))
    def _():
        index = lax.broadcasted_iota(jnp.int32, (TILE, 1), 0)
        second_row = (index >= W).astype(jnp.float32)
        column = index.astype(jnp.float32) - W * second_row - MID

        def frame(f, _):
            copies = []
            for k, src in enumerate((second, second_p, second_o, first, first_p)):
                copies.append(pltpu.make_async_copy(src.at[f], feats.at[k], sems.at[k]))
            for c in copies:
                c.start()
            for c in copies:
                c.wait()

            def job(dst, slot, query, begin, count):
                for n0 in range(0, TILE, CH):
                    w = min(CH, TILE - n0)
                    rows = feats[query, n0 : n0 + w, :]

                    def step(k, old):
                        scores = dot(feats[k], rows, NT) * SCALE
                        rel = k - begin
                        offset = jnp.where(rel == 0, 0.0, jnp.where(rel == 1, near, far))
                        use = jnp.where((rel < 2) | present, 1.0, 0.0)
                        top = jnp.max(scores, axis=0, keepdims=True)
                        weight = jnp.exp2(scores - top) * use
                        total = jnp.sum(weight, axis=0, keepdims=True)
                        fresh = (
                            jnp.where(use > 0, top, -1e30),
                            total,
                            jnp.sum(weight * column, axis=0, keepdims=True),
                            jnp.sum(weight * second_row, axis=0, keepdims=True) + offset * total,
                        )
                        return merge(old, fresh)

                    zero = jnp.zeros((1, w), jnp.float32)
                    status = (jnp.full((1, w), -1e30, jnp.float32), zero, zero, zero)
                    status = lax.fori_loop(begin, begin + count, step, status)
                    tops[f, slot : slot + 1, n0 : n0 + w] = status[0]
                    for k in range(3):
                        dst[f, k : k + 1, n0 : n0 + w] = status[1 + k]

            job(fwd, 0, 3, 0, 3)
            job(bwd, 1, 0, 3, 2)
            job(col, 2, 2, 3, 1)
            return 0

        lax.fori_loop(0, FR, frame, 0)

    def pack(f, _):
        g_o = jnp.concatenate([tops[f, 2:3, :], col[f, 0:3, :]], axis=0)
        g_i = jnp.concatenate([tops[f, 1:2, :], bwd[f, 0:3, :]], axis=0)
        o0, o1 = halves(g_o)
        i0, i1 = halves(g_i)
        flows = []
        for row, stat in enumerate(halves(fwd[f, 0:3, :])):
            fx, fy = finish(stat[0:1], stat[1:2], stat[2:3], float(row), height)
            flows.append(jnp.concatenate([fx, fy], axis=0))
        blank = jnp.zeros((2, W), jnp.float32)
        msg[f, 0:4, :] = o0
        msg[f, 4:8, :] = o1
        msg[f, 8:12, :] = jnp.where(even, i0, i1)
        msg[f, 12:14, :] = jnp.where(even, flows[0], flows[1])
        msg[f, 14:16, :] = blank
        loc[f, 0:4, :] = i0
        loc[f, 4:8, :] = i1
        loc[f, 8:10, :] = flows[0]
        loc[f, 10:12, :] = flows[1]
        return 0

    lax.fori_loop(0, FR, pack, 0)


def flow_kernel(height, loc, sent, got, rows, edge):
    even, present = side()
    far = jnp.where(even, -2.0, 2.0)

    def stat(x, offset, keep=None):
        top, total, mx, my = x[0:1], x[1:2], x[2:3], x[3:4]
        if keep is not None:
            top = jnp.where(keep, top, -1e30)
        return top, total, mx, my + offset * total

    for f in range(FR):
        maps = []
        for r in range(2):
            _, total, mx, my = merge(
                stat(loc[f, 4 * r : 4 * r + 4, :], 0.0),
                stat(got[f, 4 * r : 4 * r + 4, :], far, present),
            )
            bx, by = finish(total, mx, my, float(r), height)
            maps.append(jnp.concatenate([loc[f, 8 + 2 * r : 10 + 2 * r, :], bx, by], axis=0))
        mine = jnp.where(even, sent[f, 4:8, :], sent[f, 0:4, :])
        _, total, mx, my = merge(stat(got[f, 8:12, :], 0.0, present), stat(mine, -far))
        total = jnp.where(present, total, 1.0)
        bx, by = finish(total, mx, my, jnp.where(even, 1.0, 0.0), height)
        halo = jnp.concatenate([got[f, 12:14, :], bx, by], axis=0)
        halo = jnp.where(present, halo, 0.0)
        edge[f] = jnp.where(even, maps[1], maps[0])
        rows[f, 0:4, :] = jnp.where(even, halo, 0.0)
        rows[f, 4:8, :] = maps[0]
        rows[f, 8:12, :] = maps[1]
        rows[f, 12:16, :] = jnp.where(even, 0.0, halo)


def refine_kernel(rows, edge, taps, bias, out):
    even, _ = side()
    none = jnp.zeros((16, 1), jnp.float32)
    for f in range(FR):
        mine = rows[f]
        other = edge[f]
        full = jnp.concatenate(
            [jnp.where(even, mine[0:4], other), mine[4:12], jnp.where(even, other, mine[12:16])], axis=0
        )
        left = jnp.concatenate([none, full[:, : W - 1]], axis=1)
        right = jnp.concatenate([full[:, 1:], none], axis=1)
        patches = jnp.concatenate([left, full, right], axis=0)
        mixed = lax.dot_general(
            taps[...], patches, NN, precision=lax.Precision.HIGHEST, preferred_element_type=jnp.float32
        )
        mixed = mixed + bias[...] + full[4:12]
        for o in range(4):
            out[f, o, 0:1, :] = mixed[o : o + 1]
            out[f, o, 1:2, :] = mixed[4 + o : 5 + o]


def call(kernel, shapes, scratch, limit, flops, *args, hbm=(), far=(), alias={}):
    spec = pl.BlockSpec(memory_space=pltpu.VMEM)
    anywhere = pl.BlockSpec(memory_space=pl.ANY)
    home = pl.BlockSpec(memory_space=pltpu.HBM)
    single = not isinstance(shapes, tuple)
    return pl.pallas_call(
        kernel,
        out_shape=shapes,
        in_specs=[home if i in hbm else anywhere if i in far else spec for i in range(len(args))],
        out_specs=spec if single else (spec,) * len(shapes),
        scratch_shapes=scratch,
        input_output_aliases=alias,
        compiler_params=pltpu.CompilerParams(vmem_limit_bytes=limit << 20),
        cost_estimate=pl.CostEstimate(flops=flops, bytes_accessed=flops // 1000, transcendentals=0),
    )(*args)


def device_program(first, second, conv_weight, conv_bias):
    size = lax.axis_size("blk")
    height = 2 * size
    f32 = functools.partial(jax.ShapeDtypeStruct, dtype=jnp.float32)
    wide = pltpu.VMEM((FR, TILE, 2 * CH), jnp.bfloat16)
    plain = pltpu.VMEM((FR, TILE, CH), jnp.bfloat16)
    kept = pltpu.VMEM((FR, 8, TILE), jnp.float32)
    chip = [(i, i ^ 1) for i in range(size)]
    far = [(i, i - 1 if i % 2 == 0 else i + 1) for i in range(1, size - 1)]

    second_p = lax.ppermute(second, "blk", chip)
    first_p = lax.ppermute(first, "blk", chip)
    second_o = lax.ppermute(second, "blk", far)
    stats = f32((FR, 8, TILE))
    doubled = jax.ShapeDtypeStruct((FR, TILE, 2 * CH), jnp.bfloat16)
    own_out = (stats, stats, doubled, doubled)
    load = [plain, plain, pltpu.SemaphoreType.DMA((4,))]
    fwd, bwd, fs, ss = call(even_kernel, own_out, load, 16, 10**9, first, second, hbm=(0, 1))
    fwd, bwd, fs, ss = call(chip_kernel, own_out, [wide, wide] + load, 24, 2 * 10**9,
                            first, second, first_p, second_p, fwd, bwd, fs, ss,
                            hbm=(0, 1), alias={4: 0, 5: 1, 6: 2, 7: 3})
    scratch = [wide] + [kept] * 3 + [pltpu.VMEM((5, TILE, CH), jnp.bfloat16), kept, pltpu.SemaphoreType.DMA((5,))]
    msg, loc = call(functools.partial(far_kernel, height), (f32((FR, 16, W)),) * 2, scratch, 24, 10**9,
                    first, second, first_p, second_p, second_o, fwd, bwd, fs, hbm=(0, 1), far=(2, 3))
    got = lax.ppermute(msg, "blk", far)
    rows, edge = call(functools.partial(flow_kernel, height), (f32((FR, 16, W)), f32((FR, 4, W))), [], 4, 10**6,
                      loc, msg, got)
    other = lax.ppermute(edge, "blk", chip)
    taps = conv_weight.transpose(0, 3, 2, 1)
    taps = jnp.stack([jnp.pad(taps, ((0, 0), (0, 0), (r, 1 - r), (0, 0))) for r in range(2)])
    taps = taps.reshape(8, 48)
    bias = jnp.concatenate([conv_bias, conv_bias]).reshape(8, 1)
    return call(refine_kernel, f32((FR, 4, 2, W)), [], 4, 10**6, rows, other, taps, bias)


def solution(mesh):
    placed = (P("pair", "blk", None), P("pair", "blk", None), P(), P())
    return jax.shard_map(
        device_program,
        mesh=mesh,
        in_specs=placed,
        out_specs=P("pair", None, "blk", None),
        check_vma=False,
    )
```

```python
import functools
import math

import jax
import jax.numpy as jnp
from jax import lax
from jax.experimental import pallas as pl
from jax.experimental.pallas import tpu as pltpu
from jax.sharding import PartitionSpec as P


W = 480
TILE = 960
CH = 128
FR = 2
MID = 240.0
SCALE = math.log2(math.e) / math.sqrt(CH)
LOW = 2.0**-60
HIGH = 2.0**100
NT = (((1,), (1,)), ((), ()))
NN = (((1,), (0,)), ((), ()))


def dot(a, b, dims):
    return lax.dot_general(a, b, dims, preferred_element_type=jnp.float32)


def side():
    pos = lax.axis_index("blk")
    even = pos % 2 == 0
    present = jnp.where(even, pos > 0, pos < lax.axis_size("blk") - 1)
    return even, present


def moments():
    lane = lax.broadcasted_iota(jnp.int32, (8, TILE), 1)
    row = lax.broadcasted_iota(jnp.int32, (8, TILE), 0)
    second = (lane >= W).astype(jnp.int32)
    col = lane - W * second - int(MID)
    value = jnp.where(row == 0, 1, jnp.where(row == 1, col, jnp.where(row == 2, second, 0)))
    return value.astype(jnp.float32).astype(jnp.bfloat16)


def split_into(dst, f, feat):
    scaled = feat.astype(jnp.float32) * SCALE
    hi = scaled.astype(jnp.bfloat16)
    dst[f, :, :CH] = hi
    dst[f, :, CH:] = (scaled - hi.astype(jnp.float32)).astype(jnp.bfloat16)


def twice_into(dst, f, feat):
    dst[f, :, :CH] = feat
    dst[f, :, CH:] = feat


def down_sums(weight):
    total = ramp = later = None
    for r in range(2):
        run = None
        for g in range(r * W, (r + 1) * W, 8):
            part = weight[g : g + 8]
            run = part if run is None else run + part
            ramp = run if ramp is None else ramp + run
        total = run if total is None else total + run
        later = run
    sub = lax.broadcasted_iota(jnp.int32, total.shape, 0).astype(jnp.float32)
    col = (W - MID + sub) * total - 8.0 * ramp
    rows = [jnp.sum(v, axis=0, keepdims=True) for v in (total, col, later)]
    return jnp.concatenate(rows + [jnp.zeros((5, total.shape[1]), jnp.float32)], axis=0)


def sums(lhs, rhs, f, down, mom=None):
    size = 256 if mom is None else 512
    cuts = [(n0, min(size, TILE - n0)) for n0 in range(0, TILE, size)]

    def scores(n0, w):
        return dot(lhs[f], rhs[f, n0 : n0 + w, :], NT)

    across = None
    ahead = scores(*cuts[0])
    for i, (n0, w) in enumerate(cuts):
        weight = jnp.exp2(ahead)
        if i + 1 < len(cuts):
            ahead = scores(*cuts[i + 1])
        down(n0, w, down_sums(weight))
        if mom is not None:
            part = dot(mom[:, n0 : n0 + w], weight.astype(jnp.bfloat16), NT)
            across = part if across is None else across + part
    return across


def merge(a, b):
    top = jnp.maximum(a[0], b[0])
    ka, kb = jnp.exp2(a[0] - top), jnp.exp2(b[0] - top)
    return (top,) + tuple(u * ka + v * kb for u, v in zip(a[1:], b[1:]))


def finish(total, mom_x, mom_y, row, height):
    col = lax.broadcasted_iota(jnp.int32, total.shape, 1).astype(jnp.float32) - MID
    return (mom_x / total - col) * (2.0 / W), (mom_y / total - row) * (2.0 / height)


def own_kernel(first, second, fwd, bwd, fs, ss, fbuf, sbuf, sems):
    copies = []
    for f in range(FR):
        for k, (src, dst) in enumerate(((first, fbuf), (second, sbuf))):
            copies.append(pltpu.make_async_copy(src.at[f], dst.at[f], sems.at[2 * f + k]))
    for c in copies:
        c.start()
    mom = moments()
    for c in copies:
        c.wait()

    def frame(f, _):
        split_into(fs, f, fbuf[f])
        twice_into(ss, f, sbuf[f])

        def down(n0, w, part):
            fwd[f, :, n0 : n0 + w] = part

        bwd[f] = sums(ss, fs, f, down, mom)
        return 0

    lax.fori_loop(0, FR, frame, 0)


def shift_y(part, offset):
    row = lax.broadcasted_iota(jnp.int32, part.shape, 0)
    return part + jnp.where(row == 2, offset * part[0:1, :], 0.0)


def inside(x):
    return jnp.all((x[:, 0:1, :] >= LOW) & (x[:, 0:1, :] <= HIGH))


def exact(sources, feats, found, sems, jobs, tiles, near, far):
    index = lax.broadcasted_iota(jnp.int32, (TILE, 1), 0)
    second_row = (index >= W).astype(jnp.float32)
    column = index.astype(jnp.float32) - W * second_row - MID

    def frame(f, _):
        copies = [pltpu.make_async_copy(src.at[f], feats.at[k], sems.at[k]) for k, src in sources.items()]
        for c in copies:
            c.start()
        for c in copies:
            c.wait()

        def job(j, _):
            query = jnp.where(j == 0, 3, jnp.where(j == 1, 0, jnp.where(j == 2, 2, 5)))
            begin = jnp.where((j == 1) | (j == 2), 3, 0)
            end = begin + jnp.where(j < 2, tiles, 1)
            for n0 in range(0, TILE, CH):
                w = min(CH, TILE - n0)
                rows = feats[query, n0 : n0 + w, :]

                def step(k, old):
                    scores = dot(feats[k], rows, NT) * SCALE
                    rel = k - begin
                    offset = jnp.where(rel == 0, 0.0, jnp.where(rel == 1, near, far))
                    top = jnp.max(scores, axis=0, keepdims=True)
                    weight = jnp.exp2(scores - top)
                    total = jnp.sum(weight, axis=0, keepdims=True)
                    mom_x = jnp.sum(weight * column, axis=0, keepdims=True)
                    mom_y = jnp.sum(weight * second_row, axis=0, keepdims=True) + offset * total
                    return merge(old, (top, total, mom_x, mom_y))

                zero = jnp.zeros((1, w), jnp.float32)
                status = (jnp.full((1, w), -1e30, jnp.float32), zero, zero, zero)
                status = lax.fori_loop(begin, end, step, status)
                found[f, j, 0:4, n0 : n0 + w] = jnp.concatenate(status, axis=0)
            return 0

        lax.fori_loop(0, jobs, job, 0)
        return 0

    lax.fori_loop(0, FR, frame, 0)


def plain(part):
    return jnp.concatenate([jnp.zeros_like(part[0:1]), part[0:3]], axis=0)


def chip_kernel(first, second, first_p, second_p, fwd0, bwd0, fs, ss, fwd, bwd, part, up, fp, sp, feats, found, sems):
    even, _ = side()
    near = jnp.where(even, 2.0, -2.0)

    def frame(f, _):
        split_into(fp, f, first_p[f])
        twice_into(sp, f, second_p[f])

        def down_f(n0, w, part):
            fwd[f, :, n0 : n0 + w] = fwd0[f, :, n0 : n0 + w] + shift_y(part, near)

        def down_b(n0, w, part):
            bwd[f, :, n0 : n0 + w] = bwd0[f, :, n0 : n0 + w] + shift_y(part, near)

        sums(sp, fs, f, down_f)
        sums(fp, ss, f, down_b)
        return 0

    lax.fori_loop(0, FR, frame, 0)

    @pl.when(jnp.logical_not(even))
    def _():
        for f in range(FR):
            found[f, 0, 0:4, :] = plain(fwd[f])
            found[f, 1, 0:4, :] = plain(bwd[f])

        @pl.when(jnp.logical_not(inside(fwd) & inside(bwd)))
        def _():
            exact({0: second, 1: second_p, 3: first, 4: first_p}, feats, found, sems, 2, 2, near, near)

        for f in range(FR):
            for j in range(2):
                stat = found[f, j, 0:4, :]
                part[f, 4 * j : 4 * j + 4, :] = stat
                up[f, 4 * j : 4 * j + 4, :] = stat[:, W:]


def far_second_kernel(second_o, fs, fwd0, fwd, col, so):
    even, present = side()

    @pl.when(even & present)
    def _():
        mom = moments()

        def frame(f, _):
            twice_into(so, f, second_o[f])

            def down(n0, w, part):
                fwd[f, :, n0 : n0 + w] = fwd0[f, :, n0 : n0 + w] + shift_y(part, -2.0)

            col[f] = sums(so, fs, f, down, mom)
            return 0

        lax.fori_loop(0, FR, frame, 0)

    @pl.when(even & jnp.logical_not(present))
    def _():
        fwd[...] = fwd0[...]
        col[...] = jnp.ones_like(col)


def far_first_kernel(height, first, second, first_p, second_p, second_o, first_o, ss, bwd0, fwd, col,
                     down, flows, fo, bwd, row, feats, found, sems):
    even, present = side()

    @pl.when(even)
    def _():
        @pl.when(present)
        def _():
            mom = moments()

            def frame(f, _):
                split_into(fo, f, first_o[f])

                def keep(n0, w, part):
                    bwd[f, :, n0 : n0 + w] = bwd0[f, :, n0 : n0 + w] + shift_y(part, -2.0)

                row[f] = sums(fo, ss, f, keep, mom)
                return 0

            lax.fori_loop(0, FR, frame, 0)

        @pl.when(jnp.logical_not(present))
        def _():
            bwd[...] = bwd0[...]
            row[...] = jnp.ones_like(row)

        for f in range(FR):
            for j, stat in enumerate((fwd, bwd, col, row)):
                found[f, j, 0:4, :] = plain(stat[f])

        @pl.when(jnp.logical_not(inside(fwd) & inside(bwd) & inside(col) & inside(row)))
        def _():
            sources = {0: second, 1: second_p, 2: second_o, 3: first, 4: first_p, 5: first_o}
            exact(sources, feats, found, sems, jnp.where(present, 4, 2), jnp.where(present, 3, 2), 2.0, -2.0)

        for f in range(FR):
            for r in range(2):
                maps = []
                for j in range(2):
                    stat = found[f, j, 0:4, :]
                    stat = stat[:, r * W : r * W + W]
                    maps.extend(finish(stat[1:2], stat[2:3], stat[3:4], float(r), height))
                maps = jnp.concatenate(maps, axis=0)
                flows[f, 4 * r : 4 * r + 4, :] = maps
                if r == 0:
                    down[f, 16:20, :] = maps
            for j in range(2):
                stat = found[f, 2 + j, 0:4, :]
                down[f, 8 * j : 8 * j + 4, :] = stat[:, :W]
                down[f, 8 * j + 4 : 8 * j + 8, :] = stat[:, W:]
            down[f, 20:24, :] = jnp.zeros((4, W), jnp.float32)


def flow_kernel(height, part, flows, sent, up, down, rows, edge):
    even, present = side()

    def stat(x, offset):
        return x[0:1], x[1:2], x[2:3], x[3:4] + offset * x[1:2]

    @pl.when(even)
    def _():
        for f in range(FR):
            halo = []
            for j, mine in ((0, sent[f, 12:16, :]), (1, sent[f, 4:8, :])):
                _, total, mx, my = merge(stat(up[f, 4 * j : 4 * j + 4, :], 0.0), stat(mine, 2.0))
                halo.extend(finish(total, mx, my, 1.0, height))
            rows[f, 0:4, :] = jnp.where(present, jnp.concatenate(halo, axis=0), 0.0)
            rows[f, 4:12, :] = flows[f]
            rows[f, 12:16, :] = jnp.zeros((4, W), jnp.float32)
            edge[f] = flows[f, 4:8, :]

    @pl.when(jnp.logical_not(even))
    def _():
        for f in range(FR):
            for r in range(2):
                maps = []
                for j in range(2):
                    mine = part[f, 4 * j : 4 * j + 4, :]
                    at = 8 * (1 - j) + 4 * r
                    top, total, mx, my = stat(down[f, at : at + 4, :], 2.0)
                    other = (jnp.where(present, top, -1e30), total, mx, my)
                    _, total, mx, my = merge(stat(mine[:, r * W : r * W + W], 0.0), other)
                    maps.extend(finish(total, mx, my, float(r), height))
                maps = jnp.concatenate(maps, axis=0)
                rows[f, 4 + 4 * r : 8 + 4 * r, :] = maps
                if r == 0:
                    edge[f] = maps
            rows[f, 0:4, :] = jnp.zeros((4, W), jnp.float32)
            rows[f, 12:16, :] = jnp.where(present, down[f, 16:20, :], 0.0)


def refine_kernel(rows, edge, taps, bias, out):
    even, _ = side()
    none = jnp.zeros((16, 1), jnp.float32)
    for f in range(FR):
        mine = rows[f]
        other = edge[f]
        full = jnp.concatenate(
            [jnp.where(even, mine[0:4], other), mine[4:12], jnp.where(even, other, mine[12:16])], axis=0
        )
        left = jnp.concatenate([none, full[:, : W - 1]], axis=1)
        right = jnp.concatenate([full[:, 1:], none], axis=1)
        patches = jnp.concatenate([left, full, right], axis=0)
        mixed = lax.dot_general(
            taps[...], patches, NN, precision=lax.Precision.HIGHEST, preferred_element_type=jnp.float32
        )
        mixed = mixed + bias[...] + full[4:12]
        for o in range(4):
            out[f, o, 0:1, :] = mixed[o : o + 1]
            out[f, o, 1:2, :] = mixed[4 + o : 5 + o]


def call(kernel, shapes, scratch, limit, flops, *args, hbm=(), far=(), alias={}):
    spec = pl.BlockSpec(memory_space=pltpu.VMEM)
    anywhere = pl.BlockSpec(memory_space=pl.ANY)
    home = pl.BlockSpec(memory_space=pltpu.HBM)
    single = not isinstance(shapes, tuple)
    return pl.pallas_call(
        kernel,
        out_shape=shapes,
        in_specs=[home if i in hbm else anywhere if i in far else spec for i in range(len(args))],
        out_specs=spec if single else (spec,) * len(shapes),
        scratch_shapes=scratch,
        input_output_aliases=alias,
        compiler_params=pltpu.CompilerParams(vmem_limit_bytes=limit << 20),
        cost_estimate=pl.CostEstimate(flops=flops, bytes_accessed=flops // 1000, transcendentals=0),
    )(*args)


def device_program(first, second, conv_weight, conv_bias):
    size = lax.axis_size("blk")
    height = 2 * size
    f32 = functools.partial(jax.ShapeDtypeStruct, dtype=jnp.float32)
    wide = pltpu.VMEM((FR, TILE, 2 * CH), jnp.bfloat16)
    narrow = pltpu.VMEM((FR, TILE, CH), jnp.bfloat16)
    kept = pltpu.VMEM((FR, 8, TILE), jnp.float32)
    spare = [pltpu.VMEM((6, TILE, CH), jnp.bfloat16), pltpu.VMEM((FR, 4, 8, TILE), jnp.float32)]
    spare.append(pltpu.SemaphoreType.DMA((6,)))
    chip = [(i, i ^ 1) for i in range(size)]
    upward = [(i, i + 1) for i in range(1, size - 1, 2)]
    downward = [(j, i) for i, j in upward]

    second_o = lax.ppermute(second, "blk", upward)
    first_o = lax.ppermute(first, "blk", upward)
    second_p = lax.ppermute(second, "blk", chip)
    first_p = lax.ppermute(first, "blk", chip)
    first, second = (pltpu.with_memory_space_constraint(x, pltpu.HBM) for x in (first, second))
    stats = f32((FR, 8, TILE))
    doubled = jax.ShapeDtypeStruct((FR, TILE, 2 * CH), jnp.bfloat16)
    fwd, bwd, fs, ss = call(own_kernel, (stats, stats, doubled, doubled),
                            [narrow, narrow, pltpu.SemaphoreType.DMA((4,))], 12, 10**9,
                            first, second, hbm=(0, 1))
    fwd, bwd, part, up = call(chip_kernel, (stats, stats, stats, f32((FR, 8, W))), [wide, wide] + spare, 20,
                              2 * 10**9, first, second, first_p, second_p, fwd, bwd, fs, ss, hbm=(0, 1))
    up = lax.ppermute(up, "blk", upward)
    fwd, col = call(far_second_kernel, (stats, stats), [wide], 12, 10**9, second_o, fs, fwd)
    sent, flows = call(functools.partial(far_first_kernel, height), (f32((FR, 24, W)), f32((FR, 8, W))),
                       [wide, kept, kept] + spare, 20, 10**9,
                       first, second, first_p, second_p, second_o, first_o, ss, bwd, fwd, col,
                       hbm=(0, 1), far=(2, 3, 4))
    down = lax.ppermute(sent, "blk", downward)
    rows, edge = call(functools.partial(flow_kernel, height), (f32((FR, 16, W)), f32((FR, 4, W))), [], 4, 10**6,
                      part, flows, sent, up, down)
    other = lax.ppermute(edge, "blk", chip)
    taps = conv_weight.transpose(0, 3, 2, 1)
    taps = jnp.stack([jnp.pad(taps, ((0, 0), (0, 0), (r, 1 - r), (0, 0))) for r in range(2)])
    taps = taps.reshape(8, 48)
    bias = jnp.concatenate([conv_bias, conv_bias]).reshape(8, 1)
    return call(refine_kernel, f32((FR, 4, 2, W)), [], 4, 10**6, rows, other, taps, bias)


def solution(mesh):
    placed = (P("pair", "blk", None), P("pair", "blk", None), P(), P())
    return jax.shard_map(
        device_program,
        mesh=mesh,
        in_specs=placed,
        out_specs=P("pair", None, "blk", None),
        check_vma=False,
    )
```

```python
import functools
import math

import jax
import jax.numpy as jnp
import numpy as np
from jax import lax
from jax.experimental import pallas as pl
from jax.experimental.pallas import tpu as pltpu
from jax.sharding import PartitionSpec as P


W = 480
TILE = 960
CH = 128
FR = 2
MID = 240.0
SCALE = math.log2(math.e) / math.sqrt(CH)
LOW = 2.0**-60
HIGH = 2.0**100
NT = (((1,), (1,)), ((), ()))
NN = (((1,), (0,)), ((), ()))


def dot(a, b, dims):
    return lax.dot_general(a, b, dims, preferred_element_type=jnp.float32)


def takes(pos, size):
    upper = pos == size // 2
    return upper | ((pos % 2 == 1) & (pos != size // 2 - 1) & (pos != size - 1))


def side():
    pos, size = lax.axis_index("blk"), lax.axis_size("blk")
    even = pos % 2 == 0
    present = jnp.where(even, pos > 0, pos < size - 1)
    return even, takes(pos, size), present


def moments():
    lane = lax.broadcasted_iota(jnp.int32, (8, TILE), 1)
    row = lax.broadcasted_iota(jnp.int32, (8, TILE), 0)
    second = (lane >= W).astype(jnp.int32)
    col = lane - W * second - int(MID)
    value = jnp.where(row == 0, 1, jnp.where(row == 1, col, jnp.where(row == 2, second, 0)))
    return value.astype(jnp.float32).astype(jnp.bfloat16)


def split_into(dst, f, feat):
    scaled = feat.astype(jnp.float32) * SCALE
    hi = scaled.astype(jnp.bfloat16)
    dst[f, :, :CH] = hi
    dst[f, :, CH:] = (scaled - hi.astype(jnp.float32)).astype(jnp.bfloat16)


def twice_into(dst, f, feat):
    dst[f, :, :CH] = feat
    dst[f, :, CH:] = feat


def down_sums(weight):
    total = ramp = later = None
    for r in range(2):
        run = None
        for g in range(r * W, (r + 1) * W, 8):
            part = weight[g : g + 8]
            run = part if run is None else run + part
            ramp = run if ramp is None else ramp + run
        total = run if total is None else total + run
        later = run
    sub = lax.broadcasted_iota(jnp.int32, total.shape, 0).astype(jnp.float32)
    col = (W - MID + sub) * total - 8.0 * ramp
    rows = [jnp.sum(v, axis=0, keepdims=True) for v in (total, col, later)]
    return jnp.concatenate(rows + [jnp.zeros((5, total.shape[1]), jnp.float32)], axis=0)


def sums(lhs, rhs, f, down, mom=None):
    size = 256 if mom is None else 512
    cuts = [(n0, min(size, TILE - n0)) for n0 in range(0, TILE, size)]

    def scores(n0, w):
        return dot(lhs[f], rhs[f, n0 : n0 + w, :], NT)

    across = None
    ahead = scores(*cuts[0])
    for i, (n0, w) in enumerate(cuts):
        weight = jnp.exp2(ahead)
        if i + 1 < len(cuts):
            ahead = scores(*cuts[i + 1])
        down(n0, w, down_sums(weight))
        if mom is not None:
            part = dot(mom[:, n0 : n0 + w], weight.astype(jnp.bfloat16), NT)
            across = part if across is None else across + part
    return across


def merge(a, b):
    top = jnp.maximum(a[0], b[0])
    ka, kb = jnp.exp2(a[0] - top), jnp.exp2(b[0] - top)
    return (top,) + tuple(u * ka + v * kb for u, v in zip(a[1:], b[1:]))


def finish(total, mom_x, mom_y, row, height):
    col = lax.broadcasted_iota(jnp.int32, total.shape, 1).astype(jnp.float32) - MID
    return (mom_x / total - col) * (2.0 / W), (mom_y / total - row) * (2.0 / height)


def own_kernel(first, second, fwd, bwd, fs, ss, fbuf, sbuf, sems):
    copies = []
    for f in range(FR):
        for k, (src, dst) in enumerate(((first, fbuf), (second, sbuf))):
            copies.append(pltpu.make_async_copy(src.at[f], dst.at[f], sems.at[2 * f + k]))
    for c in copies:
        c.start()
    mom = moments()
    for c in copies:
        c.wait()

    def frame(f, _):
        split_into(fs, f, fbuf[f])
        twice_into(ss, f, sbuf[f])

        def down(n0, w, part):
            fwd[f, :, n0 : n0 + w] = part

        bwd[f] = sums(ss, fs, f, down, mom)
        return 0

    lax.fori_loop(0, FR, frame, 0)


def shift_y(part, offset):
    row = lax.broadcasted_iota(jnp.int32, part.shape, 0)
    return part + jnp.where(row == 2, offset * part[0:1, :], 0.0)


def inside(x):
    return jnp.all((x[:, 0:1, :] >= LOW) & (x[:, 0:1, :] <= HIGH))


def exact(sources, feats, found, sems, jobs, tiles, near, far):
    index = lax.broadcasted_iota(jnp.int32, (TILE, 1), 0)
    second_row = (index >= W).astype(jnp.float32)
    column = index.astype(jnp.float32) - W * second_row - MID

    def frame(f, _):
        copies = [pltpu.make_async_copy(src.at[f], feats.at[k], sems.at[k]) for k, src in sources.items()]
        for c in copies:
            c.start()
        for c in copies:
            c.wait()

        def job(j, _):
            query = jnp.where(j == 0, 3, jnp.where(j == 1, 0, jnp.where(j == 2, 2, 5)))
            begin = jnp.where((j == 1) | (j == 2), 3, 0)
            end = begin + jnp.where(j < 2, tiles, 1)
            for n0 in range(0, TILE, CH):
                w = min(CH, TILE - n0)
                rows = feats[query, n0 : n0 + w, :]

                def step(k, old):
                    scores = dot(feats[k], rows, NT) * SCALE
                    rel = k - begin
                    offset = jnp.where(rel == 0, 0.0, jnp.where(rel == 1, near, far))
                    top = jnp.max(scores, axis=0, keepdims=True)
                    weight = jnp.exp2(scores - top)
                    total = jnp.sum(weight, axis=0, keepdims=True)
                    mom_x = jnp.sum(weight * column, axis=0, keepdims=True)
                    mom_y = jnp.sum(weight * second_row, axis=0, keepdims=True) + offset * total
                    return merge(old, (top, total, mom_x, mom_y))

                zero = jnp.zeros((1, w), jnp.float32)
                status = (jnp.full((1, w), -1e30, jnp.float32), zero, zero, zero)
                status = lax.fori_loop(begin, end, step, status)
                found[f, j, 0:4, n0 : n0 + w] = jnp.concatenate(status, axis=0)
            return 0

        lax.fori_loop(0, jobs, job, 0)
        return 0

    lax.fori_loop(0, FR, frame, 0)


def plain(part):
    return jnp.concatenate([jnp.zeros_like(part[0:1]), part[0:3]], axis=0)


def chip_kernel(first, second, first_p, second_p, fwd0, bwd0, fs, ss, fwd, bwd, part, up, fp, sp, feats, found, sems):
    even, heavy, _ = side()
    near = jnp.where(even, 2.0, -2.0)

    def frame(f, _):
        split_into(fp, f, first_p[f])
        twice_into(sp, f, second_p[f])

        def down_f(n0, w, part):
            fwd[f, :, n0 : n0 + w] = fwd0[f, :, n0 : n0 + w] + shift_y(part, near)

        def down_b(n0, w, part):
            bwd[f, :, n0 : n0 + w] = bwd0[f, :, n0 : n0 + w] + shift_y(part, near)

        sums(sp, fs, f, down_f)
        sums(fp, ss, f, down_b)
        return 0

    lax.fori_loop(0, FR, frame, 0)

    @pl.when(jnp.logical_not(heavy))
    def _():
        for f in range(FR):
            found[f, 0, 0:4, :] = plain(fwd[f])
            found[f, 1, 0:4, :] = plain(bwd[f])

        @pl.when(jnp.logical_not(inside(fwd) & inside(bwd)))
        def _():
            exact({0: second, 1: second_p, 3: first, 4: first_p}, feats, found, sems, 2, 2, near, near)

        for f in range(FR):
            for j in range(2):
                stat = found[f, j, 0:4, :]
                part[f, 4 * j : 4 * j + 4, :] = stat
                up[f, 4 * j : 4 * j + 4, :] = jnp.where(even, stat[:, :W], stat[:, W:])


def far_second_kernel(second_o, fs, fwd0, fwd, col, so):
    even, heavy, _ = side()
    far = jnp.where(even, -2.0, 2.0)

    @pl.when(heavy)
    def _():
        mom = moments()

        def frame(f, _):
            twice_into(so, f, second_o[f])

            def down(n0, w, part):
                fwd[f, :, n0 : n0 + w] = fwd0[f, :, n0 : n0 + w] + shift_y(part, far)

            col[f] = sums(so, fs, f, down, mom)
            return 0

        lax.fori_loop(0, FR, frame, 0)


def far_first_kernel(height, first, second, first_p, second_p, second_o, first_o, ss, bwd0, fwd, col,
                     sent, flows, edge, fo, bwd, row, feats, found, sems):
    even, heavy, _ = side()
    far = jnp.where(even, -2.0, 2.0)

    @pl.when(heavy)
    def _():
        mom = moments()

        def frame(f, _):
            split_into(fo, f, first_o[f])

            def down(n0, w, part):
                bwd[f, :, n0 : n0 + w] = bwd0[f, :, n0 : n0 + w] + shift_y(part, far)

            row[f] = sums(fo, ss, f, down, mom)
            return 0

        lax.fori_loop(0, FR, frame, 0)
        for f in range(FR):
            for j, stat in enumerate((fwd, bwd, col, row)):
                found[f, j, 0:4, :] = plain(stat[f])

        @pl.when(jnp.logical_not(inside(fwd) & inside(bwd) & inside(col) & inside(row)))
        def _():
            sources = {0: second, 1: second_p, 2: second_o, 3: first, 4: first_p, 5: first_o}
            exact(sources, feats, found, sems, 4, 3, -far, far)

        for f in range(FR):
            maps = []
            for r in range(2):
                both = []
                for j in range(2):
                    stat = found[f, j, 0:4, :]
                    stat = stat[:, r * W : r * W + W]
                    both.extend(finish(stat[1:2], stat[2:3], stat[3:4], float(r), height))
                maps.append(jnp.concatenate(both, axis=0))
                flows[f, 4 * r : 4 * r + 4, :] = maps[r]
            edge[f] = jnp.where(even, maps[1], maps[0])
            sent[f, 16:20, :] = jnp.where(even, maps[0], maps[1])
            for j in range(2):
                stat = found[f, 2 + j, 0:4, :]
                sent[f, 8 * j : 8 * j + 4, :] = stat[:, :W]
                sent[f, 8 * j + 4 : 8 * j + 8, :] = stat[:, W:]
            sent[f, 20:24, :] = jnp.zeros((4, W), jnp.float32)


def flow_kernel(height, part, flows, sent, up, down, rows, edge):
    even, heavy, present = side()
    far = jnp.where(even, -2.0, 2.0)

    def stat(x, offset):
        return x[0:1], x[1:2], x[2:3], x[3:4] + offset * x[1:2]

    def place(f, halo):
        rows[f, 0:4, :] = jnp.where(even, halo, 0.0)
        rows[f, 12:16, :] = jnp.where(even, 0.0, halo)

    @pl.when(heavy)
    def _():
        for f in range(FR):
            halo = []
            for j in range(2):
                at = 8 * (1 - j)
                mine = jnp.where(even, sent[f, at + 4 : at + 8, :], sent[f, at : at + 4, :])
                _, total, mx, my = merge(stat(up[f, 4 * j : 4 * j + 4, :], 0.0), stat(mine, -far))
                halo.extend(finish(total, mx, my, jnp.where(even, 1.0, 0.0), height))
            place(f, jnp.concatenate(halo, axis=0))
            rows[f, 4:12, :] = flows[f]

    @pl.when(jnp.logical_not(heavy))
    def _():
        for f in range(FR):
            maps = []
            for r in range(2):
                both = []
                for j in range(2):
                    mine = part[f, 4 * j : 4 * j + 4, :]
                    at = 8 * (1 - j) + 4 * r
                    top, total, mx, my = stat(down[f, at : at + 4, :], far)
                    other = (jnp.where(present, top, -1e30), total, mx, my)
                    _, total, mx, my = merge(stat(mine[:, r * W : r * W + W], 0.0), other)
                    both.extend(finish(total, mx, my, float(r), height))
                maps.append(jnp.concatenate(both, axis=0))
                rows[f, 4 + 4 * r : 8 + 4 * r, :] = maps[r]
            edge[f] = jnp.where(even, maps[1], maps[0])
            place(f, jnp.where(present, down[f, 16:20, :], 0.0))


def refine_kernel(rows, edge_heavy, edge_light, taps, bias, out):
    even, _, _ = side()
    pos, size = lax.axis_index("blk"), lax.axis_size("blk")
    from_heavy = takes(jnp.where(even, pos + 1, pos - 1), size)
    none = jnp.zeros((16, 1), jnp.float32)
    for f in range(FR):
        mine = rows[f]
        other = jnp.where(from_heavy, edge_heavy[f], edge_light[f])
        full = jnp.concatenate(
            [jnp.where(even, mine[0:4], other), mine[4:12], jnp.where(even, other, mine[12:16])], axis=0
        )
        left = jnp.concatenate([none, full[:, : W - 1]], axis=1)
        right = jnp.concatenate([full[:, 1:], none], axis=1)
        patches = jnp.concatenate([left, full, right], axis=0)
        mixed = lax.dot_general(
            taps[...], patches, NN, precision=lax.Precision.HIGHEST, preferred_element_type=jnp.float32
        )
        mixed = mixed + bias[...] + full[4:12]
        for o in range(4):
            out[f, o, 0:1, :] = mixed[o : o + 1]
            out[f, o, 1:2, :] = mixed[4 + o : 5 + o]


def call(kernel, shapes, scratch, limit, flops, *args, hbm=(), far=(), alias={}):
    spec = pl.BlockSpec(memory_space=pltpu.VMEM)
    anywhere = pl.BlockSpec(memory_space=pl.ANY)
    home = pl.BlockSpec(memory_space=pltpu.HBM)
    single = not isinstance(shapes, tuple)
    return pl.pallas_call(
        kernel,
        out_shape=shapes,
        in_specs=[home if i in hbm else anywhere if i in far else spec for i in range(len(args))],
        out_specs=spec if single else (spec,) * len(shapes),
        scratch_shapes=scratch,
        input_output_aliases=alias,
        compiler_params=pltpu.CompilerParams(vmem_limit_bytes=limit << 20),
        cost_estimate=pl.CostEstimate(flops=flops, bytes_accessed=flops // 1000, transcendentals=0),
    )(*args)


def device_program(first, second, conv_weight, conv_bias):
    size = lax.axis_size("blk")
    height = 2 * size
    f32 = functools.partial(jax.ShapeDtypeStruct, dtype=jnp.float32)
    wide = pltpu.VMEM((FR, TILE, 2 * CH), jnp.bfloat16)
    narrow = pltpu.VMEM((FR, TILE, CH), jnp.bfloat16)
    kept = pltpu.VMEM((FR, 8, TILE), jnp.float32)
    spare = [pltpu.VMEM((6, TILE, CH), jnp.bfloat16), pltpu.VMEM((FR, 4, 8, TILE), jnp.float32)]
    spare.append(pltpu.SemaphoreType.DMA((6,)))
    chip = [(i, i ^ 1) for i in range(size)]
    heavy = [bool(takes(np.int32(i), size)) for i in range(size)]
    pairs = [(i, i + 1) for i in range(1, size - 1, 2)]
    toward = [(j, i) if heavy[i] else (i, j) for i, j in pairs]
    back = [(j, i) for i, j in toward]

    second_o = lax.ppermute(second, "blk", toward)
    first_o = lax.ppermute(first, "blk", toward)
    second_p = lax.ppermute(second, "blk", chip)
    first_p = lax.ppermute(first, "blk", chip)
    first, second = (pltpu.with_memory_space_constraint(x, pltpu.HBM) for x in (first, second))
    stats = f32((FR, 8, TILE))
    doubled = jax.ShapeDtypeStruct((FR, TILE, 2 * CH), jnp.bfloat16)
    fwd, bwd, fs, ss = call(own_kernel, (stats, stats, doubled, doubled),
                            [narrow, narrow, pltpu.SemaphoreType.DMA((4,))], 12, 10**9,
                            first, second, hbm=(0, 1))
    fwd, bwd, part, up = call(chip_kernel, (stats, stats, stats, f32((FR, 8, W))), [wide, wide] + spare, 20,
                              2 * 10**9, first, second, first_p, second_p, fwd, bwd, fs, ss, hbm=(0, 1))
    up = lax.ppermute(up, "blk", toward)
    fwd, col = call(far_second_kernel, (stats, stats), [wide], 12, 10**9, second_o, fs, fwd)
    sent, flows, edge = call(functools.partial(far_first_kernel, height),
                             (f32((FR, 24, W)), f32((FR, 8, W)), f32((FR, 4, W))),
                             [wide, kept, kept] + spare, 20, 10**9,
                             first, second, first_p, second_p, second_o, first_o, ss, bwd, fwd, col,
                             hbm=(0, 1), far=(2, 3, 4))
    down = lax.ppermute(sent, "blk", back)
    edge_heavy = lax.ppermute(edge, "blk", [c for c in chip if heavy[c[0]]])
    rows, edge = call(functools.partial(flow_kernel, height), (f32((FR, 16, W)), f32((FR, 4, W))), [], 4, 10**6,
                      part, flows, sent, up, down)
    edge_light = lax.ppermute(edge, "blk", [c for c in chip if not heavy[c[0]]])
    taps = conv_weight.transpose(0, 3, 2, 1)
    taps = jnp.stack([jnp.pad(taps, ((0, 0), (0, 0), (r, 1 - r), (0, 0))) for r in range(2)])
    taps = taps.reshape(8, 48)
    bias = jnp.concatenate([conv_bias, conv_bias]).reshape(8, 1)
    return call(refine_kernel, f32((FR, 4, 2, W)), [], 4, 10**6, rows, edge_heavy, edge_light, taps, bias)


def solution(mesh):
    placed = (P("pair", "blk", None), P("pair", "blk", None), P(), P())
    return jax.shard_map(
        device_program,
        mesh=mesh,
        in_specs=placed,
        out_specs=P("pair", None, "blk", None),
        check_vma=False,
    )
```

```python
import functools
import math

import jax
import jax.numpy as jnp
import numpy as np
from jax import lax
from jax.experimental import pallas as pl
from jax.experimental.pallas import tpu as pltpu
from jax.sharding import PartitionSpec as P


W = 480
TILE = 960
CH = 128
FR = 2
MID = 240.0
SCALE = math.log2(math.e) / math.sqrt(CH)
LOW = 2.0**-60
HIGH = 2.0**100
NT = (((1,), (1,)), ((), ()))
NN = (((1,), (0,)), ((), ()))


def dot(a, b, dims):
    return lax.dot_general(a, b, dims, preferred_element_type=jnp.float32)


def takes(pos, size):
    upper = pos == size // 2
    return upper | ((pos % 2 == 1) & (pos != size // 2 - 1) & (pos != size - 1))


def side():
    pos, size = lax.axis_index("blk"), lax.axis_size("blk")
    even = pos % 2 == 0
    present = jnp.where(even, pos > 0, pos < size - 1)
    return even, takes(pos, size), present


def moments():
    lane = lax.broadcasted_iota(jnp.int32, (8, TILE), 1)
    row = lax.broadcasted_iota(jnp.int32, (8, TILE), 0)
    second = (lane >= W).astype(jnp.int32)
    col = lane - W * second - int(MID)
    value = jnp.where(row == 0, 1, jnp.where(row == 1, col, jnp.where(row == 2, second, 0)))
    return value.astype(jnp.float32).astype(jnp.bfloat16)


def split_into(dst, f, feat):
    scaled = feat.astype(jnp.float32) * SCALE
    hi = scaled.astype(jnp.bfloat16)
    dst[f, :, :CH] = hi
    dst[f, :, CH:] = (scaled - hi.astype(jnp.float32)).astype(jnp.bfloat16)


def twice_into(dst, f, feat):
    dst[f, :, :CH] = feat
    dst[f, :, CH:] = feat


def down_sums(weight):
    total = ramp = later = None
    for r in range(2):
        run = None
        for g in range(r * W, (r + 1) * W, 8):
            part = weight[g : g + 8]
            run = part if run is None else run + part
            ramp = run if ramp is None else ramp + run
        total = run if total is None else total + run
        later = run
    sub = lax.broadcasted_iota(jnp.int32, total.shape, 0).astype(jnp.float32)
    col = (W - MID + sub) * total - 8.0 * ramp
    rows = [jnp.sum(v, axis=0, keepdims=True) for v in (total, col, later)]
    return jnp.concatenate(rows + [jnp.zeros((5, total.shape[1]), jnp.float32)], axis=0)


def sums(lhs, rhs, f, down, mom=None):
    size = 256 if mom is None else 512
    cuts = [(n0, min(size, TILE - n0)) for n0 in range(0, TILE, size)]

    def scores(n0, w):
        return dot(lhs[f], rhs[f, n0 : n0 + w, :], NT)

    across = None
    ahead = scores(*cuts[0])
    for i, (n0, w) in enumerate(cuts):
        weight = jnp.exp2(ahead)
        if i + 1 < len(cuts):
            ahead = scores(*cuts[i + 1])
        down(n0, w, down_sums(weight))
        if mom is not None:
            part = dot(mom[:, n0 : n0 + w], weight.astype(jnp.bfloat16), NT)
            across = part if across is None else across + part
    return across


def merge(a, b):
    top = jnp.maximum(a[0], b[0])
    ka, kb = jnp.exp2(a[0] - top), jnp.exp2(b[0] - top)
    return (top,) + tuple(u * ka + v * kb for u, v in zip(a[1:], b[1:]))


def finish(total, mom_x, mom_y, row, height):
    col = lax.broadcasted_iota(jnp.int32, total.shape, 1).astype(jnp.float32) - MID
    return (mom_x / total - col) * (2.0 / W), (mom_y / total - row) * (2.0 / height)


def load_kernel(first, second, both, first0, first1, sems):
    pairs = [(first.at[f], both.at[0, f]) for f in range(FR)] + [(second.at[f], both.at[1, f]) for f in range(FR)]
    pairs = [(first.at[0], first0), (first.at[1], first1)] + pairs
    copies = [pltpu.make_async_copy(src, dst, sems.at[k]) for k, (src, dst) in enumerate(pairs)]
    for c in copies:
        c.start()
    for c in copies:
        c.wait()


def own_kernel(both, fwd, bwd, fs, ss):
    mom = moments()

    def frame(f, _):
        split_into(fs, f, both[0, f])
        twice_into(ss, f, both[1, f])

        def down(n0, w, part):
            fwd[f, :, n0 : n0 + w] = part

        bwd[f] = sums(ss, fs, f, down, mom)
        return 0

    lax.fori_loop(0, FR, frame, 0)


def shift_y(part, offset):
    row = lax.broadcasted_iota(jnp.int32, part.shape, 0)
    return part + jnp.where(row == 2, offset * part[0:1, :], 0.0)


def inside(x):
    return jnp.all((x[:, 0:1, :] >= LOW) & (x[:, 0:1, :] <= HIGH))


def exact(sources, feats, found, sems, jobs, tiles, near, far):
    index = lax.broadcasted_iota(jnp.int32, (TILE, 1), 0)
    second_row = (index >= W).astype(jnp.float32)
    column = index.astype(jnp.float32) - W * second_row - MID

    def frame(f, _):
        copies = [pltpu.make_async_copy(src.at[f], feats.at[k], sems.at[k]) for k, src in sources.items()]
        for c in copies:
            c.start()
        for c in copies:
            c.wait()

        def job(j, _):
            query = jnp.where(j == 0, 3, jnp.where(j == 1, 0, jnp.where(j == 2, 2, 5)))
            begin = jnp.where((j == 1) | (j == 2), 3, 0)
            end = begin + jnp.where(j < 2, tiles, 1)
            for n0 in range(0, TILE, CH):
                w = min(CH, TILE - n0)
                rows = feats[query, n0 : n0 + w, :]

                def step(k, old):
                    scores = dot(feats[k], rows, NT) * SCALE
                    rel = k - begin
                    offset = jnp.where(rel == 0, 0.0, jnp.where(rel == 1, near, far))
                    top = jnp.max(scores, axis=0, keepdims=True)
                    weight = jnp.exp2(scores - top)
                    total = jnp.sum(weight, axis=0, keepdims=True)
                    mom_x = jnp.sum(weight * column, axis=0, keepdims=True)
                    mom_y = jnp.sum(weight * second_row, axis=0, keepdims=True) + offset * total
                    return merge(old, (top, total, mom_x, mom_y))

                zero = jnp.zeros((1, w), jnp.float32)
                status = (jnp.full((1, w), -1e30, jnp.float32), zero, zero, zero)
                status = lax.fori_loop(begin, end, step, status)
                found[f, j, 0:4, n0 : n0 + w] = jnp.concatenate(status, axis=0)
            return 0

        lax.fori_loop(0, jobs, job, 0)
        return 0

    lax.fori_loop(0, FR, frame, 0)


def tiles_of(both, both_p):
    return {0: both.at[1], 1: both_p.at[1], 3: both.at[0], 4: both_p.at[0]}


def plain(part):
    return jnp.concatenate([jnp.zeros_like(part[0:1]), part[0:3]], axis=0)


def chip_kernel(both, both_p, fwd0, bwd0, fs, fwd, bwd, part, up, ss, fp, sp, feats, found, sems):
    even, heavy, _ = side()
    near = jnp.where(even, 2.0, -2.0)

    def frame(f, _):
        twice_into(ss, f, both[1, f])
        split_into(fp, f, both_p[0, f])
        twice_into(sp, f, both_p[1, f])

        def down_f(n0, w, part):
            fwd[f, :, n0 : n0 + w] = fwd0[f, :, n0 : n0 + w] + shift_y(part, near)

        def down_b(n0, w, part):
            bwd[f, :, n0 : n0 + w] = bwd0[f, :, n0 : n0 + w] + shift_y(part, near)

        sums(sp, fs, f, down_f)
        sums(fp, ss, f, down_b)
        return 0

    lax.fori_loop(0, FR, frame, 0)

    @pl.when(jnp.logical_not(heavy))
    def _():
        for f in range(FR):
            found[f, 0, 0:4, :] = plain(fwd[f])
            found[f, 1, 0:4, :] = plain(bwd[f])

        @pl.when(jnp.logical_not(inside(fwd) & inside(bwd)))
        def _():
            exact(tiles_of(both, both_p), feats, found, sems, 2, 2, near, near)

        for f in range(FR):
            for j in range(2):
                stat = found[f, j, 0:4, :]
                part[f, 4 * j : 4 * j + 4, :] = stat
                up[f, 4 * j : 4 * j + 4, :] = jnp.where(even, stat[:, :W], stat[:, W:])


def far_second_kernel(second_o, fs, fwd0, taps, bias, fwd, col, so):
    even, heavy, _ = side()
    far = jnp.where(even, -2.0, 2.0)

    @pl.when(heavy)
    def _():
        mom = moments()

        def frame(f, _):
            twice_into(so, f, second_o[f])

            def down(n0, w, part):
                fwd[f, :, n0 : n0 + w] = fwd0[f, :, n0 : n0 + w] + shift_y(part, far)

            col[f] = sums(so, fs, f, down, mom)
            return 0

        lax.fori_loop(0, FR, frame, 0)


def far_first(f, first_o, both, bwd0, bwd, row, fo, ss, far):
    split_into(fo, 0, first_o[...])
    twice_into(ss, 0, both[1, f])

    def down(n0, w, part):
        bwd[:, n0 : n0 + w] = bwd0[f, :, n0 : n0 + w] + shift_y(part, far)

    row[...] = sums(fo, ss, 0, down, moments())


def far_first0_kernel(first_o, both, bwd0, bwd, row, fo, ss):
    even, heavy, _ = side()

    @pl.when(heavy)
    def _():
        far_first(0, first_o, both, bwd0, bwd, row, fo, ss, jnp.where(even, -2.0, 2.0))


def far_first1_kernel(height, both, both_p, second_o, first_o0, first_o1, bwd0, fwd, col, bwd1, row1,
                      sent, flows, edge, fo, ss, bwd, row, feats, found, stage, sems):
    even, heavy, _ = side()
    far = jnp.where(even, -2.0, 2.0)

    @pl.when(heavy)
    def _():
        bwd[0] = bwd1[...]
        row[0] = row1[...]
        far_first(1, first_o1, both, bwd0, bwd.at[1], row.at[1], fo, ss, far)
        for f in range(FR):
            for j, stat in enumerate((fwd, bwd, col, row)):
                found[f, j, 0:4, :] = plain(stat[f])

        @pl.when(jnp.logical_not(inside(fwd) & inside(bwd) & inside(col) & inside(row)))
        def _():
            copies = [
                pltpu.make_async_copy(src, stage.at[f], sems.at[f]) for f, src in enumerate((first_o0, first_o1))
            ]
            for c in copies:
                c.start()
            for c in copies:
                c.wait()
            sources = {**tiles_of(both, both_p), 2: second_o, 5: stage}
            exact(sources, feats, found, sems, 4, 3, -far, far)

        for f in range(FR):
            maps = []
            for r in range(2):
                pieces = []
                for j in range(2):
                    stat = found[f, j, 0:4, :]
                    stat = stat[:, r * W : r * W + W]
                    pieces.extend(finish(stat[1:2], stat[2:3], stat[3:4], float(r), height))
                maps.append(jnp.concatenate(pieces, axis=0))
                flows[f, 4 * r : 4 * r + 4, :] = maps[r]
            edge[f] = jnp.where(even, maps[1], maps[0])
            sent[f, 16:20, :] = jnp.where(even, maps[0], maps[1])
            for j in range(2):
                stat = found[f, 2 + j, 0:4, :]
                sent[f, 8 * j : 8 * j + 4, :] = stat[:, :W]
                sent[f, 8 * j + 4 : 8 * j + 8, :] = stat[:, W:]
            sent[f, 20:24, :] = jnp.zeros((4, W), jnp.float32)


def flow_kernel(height, part, flows, sent, up, down, rows, edge):
    even, heavy, present = side()
    far = jnp.where(even, -2.0, 2.0)

    def stat(x, offset):
        return x[0:1], x[1:2], x[2:3], x[3:4] + offset * x[1:2]

    def place(f, halo):
        rows[f, 0:4, :] = jnp.where(even, halo, 0.0)
        rows[f, 12:16, :] = jnp.where(even, 0.0, halo)

    @pl.when(heavy)
    def _():
        for f in range(FR):
            halo = []
            for j in range(2):
                at = 8 * (1 - j)
                mine = jnp.where(even, sent[f, at + 4 : at + 8, :], sent[f, at : at + 4, :])
                _, total, mx, my = merge(stat(up[f, 4 * j : 4 * j + 4, :], 0.0), stat(mine, -far))
                halo.extend(finish(total, mx, my, jnp.where(even, 1.0, 0.0), height))
            place(f, jnp.concatenate(halo, axis=0))
            rows[f, 4:12, :] = flows[f]

    @pl.when(jnp.logical_not(heavy))
    def _():
        for f in range(FR):
            maps = []
            for r in range(2):
                pieces = []
                for j in range(2):
                    mine = part[f, 4 * j : 4 * j + 4, :]
                    at = 8 * (1 - j) + 4 * r
                    top, total, mx, my = stat(down[f, at : at + 4, :], far)
                    other = (jnp.where(present, top, -1e30), total, mx, my)
                    _, total, mx, my = merge(stat(mine[:, r * W : r * W + W], 0.0), other)
                    pieces.extend(finish(total, mx, my, float(r), height))
                maps.append(jnp.concatenate(pieces, axis=0))
                rows[f, 4 + 4 * r : 8 + 4 * r, :] = maps[r]
            edge[f] = jnp.where(even, maps[1], maps[0])
            place(f, jnp.where(present, down[f, 16:20, :], 0.0))


def refine_kernel(rows, edge_heavy, edge_light, taps, bias, out):
    even, _, _ = side()
    pos, size = lax.axis_index("blk"), lax.axis_size("blk")
    from_heavy = takes(jnp.where(even, pos + 1, pos - 1), size)
    none = jnp.zeros((16, 1), jnp.float32)
    for f in range(FR):
        mine = rows[f]
        other = jnp.where(from_heavy, edge_heavy[f], edge_light[f])
        full = jnp.concatenate(
            [jnp.where(even, mine[0:4], other), mine[4:12], jnp.where(even, other, mine[12:16])], axis=0
        )
        left = jnp.concatenate([none, full[:, : W - 1]], axis=1)
        right = jnp.concatenate([full[:, 1:], none], axis=1)
        patches = jnp.concatenate([left, full, right], axis=0)
        mixed = lax.dot_general(
            taps[...], patches, NN, precision=lax.Precision.HIGHEST, preferred_element_type=jnp.float32
        )
        mixed = mixed + bias[...] + full[4:12]
        for o in range(4):
            out[f, o, 0:1, :] = mixed[o : o + 1]
            out[f, o, 1:2, :] = mixed[4 + o : 5 + o]


def call(kernel, shapes, scratch, limit, flops, *args, hbm=(), far=()):
    spec = pl.BlockSpec(memory_space=pltpu.VMEM)
    anywhere = pl.BlockSpec(memory_space=pl.ANY)
    home = pl.BlockSpec(memory_space=pltpu.HBM)
    single = not isinstance(shapes, tuple)
    return pl.pallas_call(
        kernel,
        out_shape=shapes,
        in_specs=[home if i in hbm else anywhere if i in far else spec for i in range(len(args))],
        out_specs=spec if single else (spec,) * len(shapes),
        scratch_shapes=scratch,
        compiler_params=pltpu.CompilerParams(vmem_limit_bytes=limit << 20),
        cost_estimate=pl.CostEstimate(flops=flops, bytes_accessed=flops // 1000, transcendentals=0),
    )(*args)


def device_program(first, second, conv_weight, conv_bias):
    size = lax.axis_size("blk")
    height = 2 * size
    f32 = functools.partial(jax.ShapeDtypeStruct, dtype=jnp.float32)
    wide = pltpu.VMEM((FR, TILE, 2 * CH), jnp.bfloat16)
    narrow = pltpu.VMEM((FR, TILE, CH), jnp.bfloat16)
    kept = pltpu.VMEM((FR, 8, TILE), jnp.float32)
    spare = [pltpu.VMEM((6, TILE, CH), jnp.bfloat16), pltpu.VMEM((FR, 4, 8, TILE), jnp.float32)]
    spare.append(pltpu.SemaphoreType.DMA((6,)))
    chip = [(i, i ^ 1) for i in range(size)]
    heavy = [bool(takes(np.int32(i), size)) for i in range(size)]
    pairs = [(i, i + 1) for i in range(1, size - 1, 2)]
    toward = [(j, i) if heavy[i] else (i, j) for i, j in pairs]
    back = [(j, i) for i, j in toward]

    taps = conv_weight.transpose(0, 3, 2, 1)
    taps = jnp.stack([jnp.pad(taps, ((0, 0), (0, 0), (r, 1 - r), (0, 0))) for r in range(2)])
    taps = taps.reshape(8, 48)
    bias = jnp.concatenate([conv_bias, conv_bias]).reshape(8, 1)
    second_o = lax.ppermute(second, "blk", toward)
    first, second = (pltpu.with_memory_space_constraint(x, pltpu.HBM) for x in (first, second))
    tile = jax.ShapeDtypeStruct((TILE, CH), jnp.bfloat16)
    loaded = jax.ShapeDtypeStruct((2, FR, TILE, CH), jnp.bfloat16)
    both, first0, first1 = call(load_kernel, (loaded, tile, tile), [pltpu.SemaphoreType.DMA((6,))], 4, 10**6,
                                first, second, hbm=(0, 1))
    first_o0 = lax.ppermute(first0, "blk", toward)
    first_o1 = lax.ppermute(first1, "blk", toward)
    both_p = lax.ppermute(both, "blk", chip)
    stats, frame = f32((FR, 8, TILE)), f32((8, TILE))
    doubled = jax.ShapeDtypeStruct((FR, TILE, 2 * CH), jnp.bfloat16)
    own_out = (stats, stats, doubled)
    fwd, bwd, fs = call(own_kernel, own_out, [wide], 8, 10**9, both)
    fwd, bwd, part, up = call(chip_kernel, (stats, stats, stats, f32((FR, 8, W))), [wide] * 3 + spare, 16,
                              2 * 10**9, both, both_p, fwd, bwd, fs)
    up = lax.ppermute(up, "blk", toward)
    fwd, col = call(far_second_kernel, (stats, stats), [wide], 8, 10**9, second_o, fs, fwd, taps, bias)
    single = pltpu.VMEM((1, TILE, 2 * CH), jnp.bfloat16)
    bwd1, row1 = call(far_first0_kernel, (frame, frame), [single] * 2, 8, 5 * 10**8, first_o0, both, bwd)
    sent, flows, edge = call(functools.partial(far_first1_kernel, height),
                             (f32((FR, 24, W)), f32((FR, 8, W)), f32((FR, 4, W))),
                             [single, single, kept, kept] + spare[:2] + [narrow] + spare[2:], 12, 5 * 10**8,
                             both, both_p, second_o, first_o0, first_o1, bwd, fwd, col, bwd1, row1,
                             far=(1, 2))
    down = lax.ppermute(sent, "blk", back)
    edge_heavy = lax.ppermute(edge, "blk", [c for c in chip if heavy[c[0]]])
    rows, edge = call(functools.partial(flow_kernel, height), (f32((FR, 16, W)), f32((FR, 4, W))), [], 4, 10**6,
                      part, flows, sent, up, down)
    edge_light = lax.ppermute(edge, "blk", [c for c in chip if not heavy[c[0]]])
    return call(refine_kernel, f32((FR, 4, 2, W)), [], 4, 10**6, rows, edge_heavy, edge_light, taps, bias)


def solution(mesh):
    placed = (P("pair", "blk", None), P("pair", "blk", None), P(), P())
    return jax.shard_map(
        device_program,
        mesh=mesh,
        in_specs=placed,
        out_specs=P("pair", None, "blk", None),
        check_vma=False,
    )
```

```python
import functools
import math

import jax
import jax.numpy as jnp
import numpy as np
from jax import lax
from jax.experimental import pallas as pl
from jax.experimental.pallas import tpu as pltpu
from jax.sharding import PartitionSpec as P


W = 480
TILE = 960
CH = 128
FR = 2
MID = 240.0
SCALE = math.log2(math.e) / math.sqrt(CH)
LOW = 2.0**-60
HIGH = 2.0**100
NT = (((1,), (1,)), ((), ()))
NN = (((1,), (0,)), ((), ()))


def dot(a, b, dims):
    return lax.dot_general(a, b, dims, preferred_element_type=jnp.float32)


def takes(pos, size):
    upper = pos == size // 2
    return upper | ((pos % 2 == 1) & (pos != size // 2 - 1) & (pos != size - 1))


def side():
    pos, size = lax.axis_index("blk"), lax.axis_size("blk")
    even = pos % 2 == 0
    present = jnp.where(even, pos > 0, pos < size - 1)
    return even, takes(pos, size), present


def moments():
    lane = lax.broadcasted_iota(jnp.int32, (8, TILE), 1)
    row = lax.broadcasted_iota(jnp.int32, (8, TILE), 0)
    second = (lane >= W).astype(jnp.int32)
    col = lane - W * second - int(MID)
    value = jnp.where(row == 0, 1, jnp.where(row == 1, col, jnp.where(row == 2, second, 0)))
    return value.astype(jnp.float32).astype(jnp.bfloat16)


def split_into(dst, f, feat):
    scaled = feat.astype(jnp.float32) * SCALE
    hi = scaled.astype(jnp.bfloat16)
    dst[f, :, :CH] = hi
    dst[f, :, CH:] = (scaled - hi.astype(jnp.float32)).astype(jnp.bfloat16)


def twice_into(dst, f, feat):
    dst[f, :, :CH] = feat
    dst[f, :, CH:] = feat


def down_sums(weight):
    total = ramp = later = None
    for r in range(2):
        run = None
        for g in range(r * W, (r + 1) * W, 8):
            part = weight[g : g + 8]
            run = part if run is None else run + part
            ramp = run if ramp is None else ramp + run
        total = run if total is None else total + run
        later = run
    sub = lax.broadcasted_iota(jnp.int32, total.shape, 0).astype(jnp.float32)
    col = (W - MID + sub) * total - 8.0 * ramp
    rows = [jnp.sum(v, axis=0, keepdims=True) for v in (total, col, later)]
    return jnp.concatenate(rows + [jnp.zeros((5, total.shape[1]), jnp.float32)], axis=0)


def sums(lhs, rhs, f, down, mom=None):
    size = 256 if mom is None else 512
    cuts = [(n0, min(size, TILE - n0)) for n0 in range(0, TILE, size)]

    def scores(n0, w):
        return dot(lhs[f], rhs[f, n0 : n0 + w, :], NT)

    across = None
    ahead = scores(*cuts[0])
    for i, (n0, w) in enumerate(cuts):
        weight = jnp.exp2(ahead)
        if i + 1 < len(cuts):
            ahead = scores(*cuts[i + 1])
        down(n0, w, down_sums(weight))
        if mom is not None:
            part = dot(mom[:, n0 : n0 + w], weight.astype(jnp.bfloat16), NT)
            across = part if across is None else across + part
    return across


def merge(a, b):
    top = jnp.maximum(a[0], b[0])
    ka, kb = jnp.exp2(a[0] - top), jnp.exp2(b[0] - top)
    return (top,) + tuple(u * ka + v * kb for u, v in zip(a[1:], b[1:]))


def finish(total, mom_x, mom_y, row, height):
    col = lax.broadcasted_iota(jnp.int32, total.shape, 1).astype(jnp.float32) - MID
    return (mom_x / total - col) * (2.0 / W), (mom_y / total - row) * (2.0 / height)


def load_kernel(first, second, both, first0, first1, sems):
    pairs = [(first.at[f], both.at[0, f]) for f in range(FR)] + [(second.at[f], both.at[1, f]) for f in range(FR)]
    copies = [pltpu.make_async_copy(src, dst, sems.at[k]) for k, (src, dst) in enumerate(pairs)]
    for c in copies:
        c.start()
    for c in copies:
        c.wait()
    first0[...] = both[0, 0]
    first1[...] = both[0, 1]


def own_kernel(both, fwd, bwd, fs, ss):
    mom = moments()

    def frame(f, _):
        split_into(fs, f, both[0, f])
        twice_into(ss, f, both[1, f])

        def down(n0, w, part):
            fwd[f, :, n0 : n0 + w] = part

        bwd[f] = sums(ss, fs, f, down, mom)
        return 0

    lax.fori_loop(0, FR, frame, 0)


def shift_y(part, offset):
    row = lax.broadcasted_iota(jnp.int32, part.shape, 0)
    return part + jnp.where(row == 2, offset * part[0:1, :], 0.0)


def inside(x):
    return jnp.all((x[:, 0:1, :] >= LOW) & (x[:, 0:1, :] <= HIGH))


def exact(sources, feats, found, sems, jobs, tiles, near, far):
    index = lax.broadcasted_iota(jnp.int32, (TILE, 1), 0)
    second_row = (index >= W).astype(jnp.float32)
    column = index.astype(jnp.float32) - W * second_row - MID

    def frame(f, _):
        copies = [pltpu.make_async_copy(src.at[f], feats.at[k], sems.at[k]) for k, src in sources.items()]
        for c in copies:
            c.start()
        for c in copies:
            c.wait()

        def job(j, _):
            query = jnp.where(j == 0, 3, jnp.where(j == 1, 0, jnp.where(j == 2, 2, 5)))
            begin = jnp.where((j == 1) | (j == 2), 3, 0)
            end = begin + jnp.where(j < 2, tiles, 1)
            for n0 in range(0, TILE, CH):
                w = min(CH, TILE - n0)
                rows = feats[query, n0 : n0 + w, :]

                def step(k, old):
                    scores = dot(feats[k], rows, NT) * SCALE
                    rel = k - begin
                    offset = jnp.where(rel == 0, 0.0, jnp.where(rel == 1, near, far))
                    top = jnp.max(scores, axis=0, keepdims=True)
                    weight = jnp.exp2(scores - top)
                    total = jnp.sum(weight, axis=0, keepdims=True)
                    mom_x = jnp.sum(weight * column, axis=0, keepdims=True)
                    mom_y = jnp.sum(weight * second_row, axis=0, keepdims=True) + offset * total
                    return merge(old, (top, total, mom_x, mom_y))

                zero = jnp.zeros((1, w), jnp.float32)
                status = (jnp.full((1, w), -1e30, jnp.float32), zero, zero, zero)
                status = lax.fori_loop(begin, end, step, status)
                found[f, j, 0:4, n0 : n0 + w] = jnp.concatenate(status, axis=0)
            return 0

        lax.fori_loop(0, jobs, job, 0)
        return 0

    lax.fori_loop(0, FR, frame, 0)


def tiles_of(both, both_p):
    return {0: both.at[1], 1: both_p.at[1], 3: both.at[0], 4: both_p.at[0]}


def plain(part):
    return jnp.concatenate([jnp.zeros_like(part[0:1]), part[0:3]], axis=0)


def chip_kernel(both, both_p, fwd0, bwd0, fs, fwd, bwd, part, up, ss, fp, sp, feats, found, sems):
    even, heavy, _ = side()
    near = jnp.where(even, 2.0, -2.0)

    def frame(f, _):
        twice_into(ss, f, both[1, f])
        split_into(fp, f, both_p[0, f])
        twice_into(sp, f, both_p[1, f])

        def down_f(n0, w, part):
            fwd[f, :, n0 : n0 + w] = fwd0[f, :, n0 : n0 + w] + shift_y(part, near)

        def down_b(n0, w, part):
            bwd[f, :, n0 : n0 + w] = bwd0[f, :, n0 : n0 + w] + shift_y(part, near)

        sums(sp, fs, f, down_f)
        sums(fp, ss, f, down_b)
        return 0

    lax.fori_loop(0, FR, frame, 0)

    @pl.when(jnp.logical_not(heavy))
    def _():
        for f in range(FR):
            found[f, 0, 0:4, :] = plain(fwd[f])
            found[f, 1, 0:4, :] = plain(bwd[f])

        @pl.when(jnp.logical_not(inside(fwd) & inside(bwd)))
        def _():
            exact(tiles_of(both, both_p), feats, found, sems, 2, 2, near, near)

        for f in range(FR):
            for j in range(2):
                stat = found[f, j, 0:4, :]
                part[f, 4 * j : 4 * j + 4, :] = stat
                up[f, 4 * j : 4 * j + 4, :] = jnp.where(even, stat[:, :W], stat[:, W:])


def far_second_kernel(second_o, fs, fwd0, taps, bias, fwd, col, so):
    even, heavy, _ = side()
    far = jnp.where(even, -2.0, 2.0)

    @pl.when(heavy)
    def _():
        mom = moments()

        def frame(f, _):
            twice_into(so, f, second_o[f])

            def down(n0, w, part):
                fwd[f, :, n0 : n0 + w] = fwd0[f, :, n0 : n0 + w] + shift_y(part, far)

            col[f] = sums(so, fs, f, down, mom)
            return 0

        lax.fori_loop(0, FR, frame, 0)


def far_first(f, first_o, both, bwd0, bwd, row, fo, ss, far):
    split_into(fo, 0, first_o[...])
    twice_into(ss, 0, both[1, f])

    def down(n0, w, part):
        bwd[:, n0 : n0 + w] = bwd0[f, :, n0 : n0 + w] + shift_y(part, far)

    row[...] = sums(fo, ss, 0, down, moments())


def far_first0_kernel(first_o, both, bwd0, bwd, row, fo, ss):
    even, heavy, _ = side()

    @pl.when(heavy)
    def _():
        far_first(0, first_o, both, bwd0, bwd, row, fo, ss, jnp.where(even, -2.0, 2.0))


def far_first1_kernel(height, both, both_p, second_o, first_o0, first_o1, bwd0, fwd, col, bwd1, row1, part,
                      sent, flows, edge, fo, ss, bwd, row, feats, found, stage, sems):
    even, heavy, present = side()
    far = jnp.where(even, -2.0, 2.0)

    @pl.when(jnp.logical_not(present))
    def _():
        for f in range(FR):
            pieces = []
            for j in range(2):
                stat = part[f, 4 * j : 4 * j + 4, :]
                stat = jnp.where(even, stat[:, W:], stat[:, :W])
                pieces.extend(finish(stat[1:2], stat[2:3], stat[3:4], jnp.where(even, 1.0, 0.0), height))
            edge[f] = jnp.concatenate(pieces, axis=0)

    @pl.when(heavy)
    def _():
        bwd[0] = bwd1[...]
        row[0] = row1[...]
        far_first(1, first_o1, both, bwd0, bwd.at[1], row.at[1], fo, ss, far)
        for f in range(FR):
            for j, stat in enumerate((fwd, bwd, col, row)):
                found[f, j, 0:4, :] = plain(stat[f])

        @pl.when(jnp.logical_not(inside(fwd) & inside(bwd) & inside(col) & inside(row)))
        def _():
            copies = [
                pltpu.make_async_copy(src, stage.at[f], sems.at[f]) for f, src in enumerate((first_o0, first_o1))
            ]
            for c in copies:
                c.start()
            for c in copies:
                c.wait()
            sources = {**tiles_of(both, both_p), 2: second_o, 5: stage}
            exact(sources, feats, found, sems, 4, 3, -far, far)

        for f in range(FR):
            maps = []
            for r in range(2):
                pieces = []
                for j in range(2):
                    stat = found[f, j, 0:4, :]
                    stat = stat[:, r * W : r * W + W]
                    pieces.extend(finish(stat[1:2], stat[2:3], stat[3:4], float(r), height))
                maps.append(jnp.concatenate(pieces, axis=0))
                flows[f, 4 * r : 4 * r + 4, :] = maps[r]
            edge[f] = jnp.where(even, maps[1], maps[0])
            sent[f, 16:20, :] = jnp.where(even, maps[0], maps[1])
            for j in range(2):
                stat = found[f, 2 + j, 0:4, :]
                sent[f, 8 * j : 8 * j + 4, :] = stat[:, :W]
                sent[f, 8 * j + 4 : 8 * j + 8, :] = stat[:, W:]
            sent[f, 20:24, :] = jnp.zeros((4, W), jnp.float32)


def flow_kernel(height, part, flows, sent, up, down, rows, edge):
    even, heavy, present = side()
    far = jnp.where(even, -2.0, 2.0)

    def stat(x, offset):
        return x[0:1], x[1:2], x[2:3], x[3:4] + offset * x[1:2]

    def place(f, halo):
        rows[f, 0:4, :] = jnp.where(even, halo, 0.0)
        rows[f, 12:16, :] = jnp.where(even, 0.0, halo)

    @pl.when(heavy)
    def _():
        for f in range(FR):
            halo = []
            for j in range(2):
                at = 8 * (1 - j)
                mine = jnp.where(even, sent[f, at + 4 : at + 8, :], sent[f, at : at + 4, :])
                _, total, mx, my = merge(stat(up[f, 4 * j : 4 * j + 4, :], 0.0), stat(mine, -far))
                halo.extend(finish(total, mx, my, jnp.where(even, 1.0, 0.0), height))
            place(f, jnp.concatenate(halo, axis=0))
            rows[f, 4:12, :] = flows[f]

    @pl.when(jnp.logical_not(heavy))
    def _():
        for f in range(FR):
            maps = []
            for r in range(2):
                pieces = []
                for j in range(2):
                    mine = part[f, 4 * j : 4 * j + 4, :]
                    at = 8 * (1 - j) + 4 * r
                    top, total, mx, my = stat(down[f, at : at + 4, :], far)
                    other = (jnp.where(present, top, -1e30), total, mx, my)
                    _, total, mx, my = merge(stat(mine[:, r * W : r * W + W], 0.0), other)
                    pieces.extend(finish(total, mx, my, float(r), height))
                maps.append(jnp.concatenate(pieces, axis=0))
                rows[f, 4 + 4 * r : 8 + 4 * r, :] = maps[r]
            edge[f] = jnp.where(even, maps[1], maps[0])
            place(f, jnp.where(present, down[f, 16:20, :], 0.0))


def refine_kernel(rows, edge_heavy, edge_light, taps, bias, out):
    even, _, _ = side()
    pos, size = lax.axis_index("blk"), lax.axis_size("blk")
    partner = jnp.where(even, pos + 1, pos - 1)
    from_heavy = takes(partner, size) | (partner == 0) | (partner == size - 1)
    none = jnp.zeros((16, 1), jnp.float32)
    for f in range(FR):
        mine = rows[f]
        other = jnp.where(from_heavy, edge_heavy[f], edge_light[f])
        full = jnp.concatenate(
            [jnp.where(even, mine[0:4], other), mine[4:12], jnp.where(even, other, mine[12:16])], axis=0
        )
        left = jnp.concatenate([none, full[:, : W - 1]], axis=1)
        right = jnp.concatenate([full[:, 1:], none], axis=1)
        patches = jnp.concatenate([left, full, right], axis=0)
        mixed = lax.dot_general(
            taps[...], patches, NN, precision=lax.Precision.HIGHEST, preferred_element_type=jnp.float32
        )
        mixed = mixed + bias[...] + full[4:12]
        for o in range(4):
            out[f, o, 0:1, :] = mixed[o : o + 1]
            out[f, o, 1:2, :] = mixed[4 + o : 5 + o]


def call(kernel, shapes, scratch, limit, flops, *args, hbm=(), far=()):
    spec = pl.BlockSpec(memory_space=pltpu.VMEM)
    anywhere = pl.BlockSpec(memory_space=pl.ANY)
    home = pl.BlockSpec(memory_space=pltpu.HBM)
    single = not isinstance(shapes, tuple)
    return pl.pallas_call(
        kernel,
        out_shape=shapes,
        in_specs=[home if i in hbm else anywhere if i in far else spec for i in range(len(args))],
        out_specs=spec if single else (spec,) * len(shapes),
        scratch_shapes=scratch,
        compiler_params=pltpu.CompilerParams(vmem_limit_bytes=limit << 20),
        cost_estimate=pl.CostEstimate(flops=flops, bytes_accessed=flops // 1000, transcendentals=0),
    )(*args)


def device_program(first, second, conv_weight, conv_bias):
    size = lax.axis_size("blk")
    height = 2 * size
    f32 = functools.partial(jax.ShapeDtypeStruct, dtype=jnp.float32)
    wide = pltpu.VMEM((FR, TILE, 2 * CH), jnp.bfloat16)
    narrow = pltpu.VMEM((FR, TILE, CH), jnp.bfloat16)
    kept = pltpu.VMEM((FR, 8, TILE), jnp.float32)
    spare = [pltpu.VMEM((6, TILE, CH), jnp.bfloat16), pltpu.VMEM((FR, 4, 8, TILE), jnp.float32)]
    spare.append(pltpu.SemaphoreType.DMA((6,)))
    chip = [(i, i ^ 1) for i in range(size)]
    heavy = [bool(takes(np.int32(i), size)) for i in range(size)]
    pairs = [(i, i + 1) for i in range(1, size - 1, 2)]
    toward = [(j, i) if heavy[i] else (i, j) for i, j in pairs]
    back = [(j, i) for i, j in toward]
    early = [heavy[i] or i in (0, size - 1) for i in range(size)]

    taps = conv_weight.transpose(0, 3, 2, 1)
    taps = jnp.stack([jnp.pad(taps, ((0, 0), (0, 0), (r, 1 - r), (0, 0))) for r in range(2)])
    taps = taps.reshape(8, 48)
    bias = jnp.concatenate([conv_bias, conv_bias]).reshape(8, 1)
    second_o = lax.ppermute(second, "blk", toward)
    first, second = (pltpu.with_memory_space_constraint(x, pltpu.HBM) for x in (first, second))
    tile = jax.ShapeDtypeStruct((TILE, CH), jnp.bfloat16)
    loaded = jax.ShapeDtypeStruct((2, FR, TILE, CH), jnp.bfloat16)
    both, first0, first1 = call(load_kernel, (loaded, tile, tile), [pltpu.SemaphoreType.DMA((4,))], 4, 10**6,
                                first, second, hbm=(0, 1))
    first_o0 = lax.ppermute(first0, "blk", toward)
    first_o1 = lax.ppermute(first1, "blk", toward)
    both_p = lax.ppermute(both, "blk", chip)
    stats, frame = f32((FR, 8, TILE)), f32((8, TILE))
    doubled = jax.ShapeDtypeStruct((FR, TILE, 2 * CH), jnp.bfloat16)
    own_out = (stats, stats, doubled)
    fwd, bwd, fs = call(own_kernel, own_out, [wide], 8, 10**9, both)
    fwd, bwd, part, up = call(chip_kernel, (stats, stats, stats, f32((FR, 8, W))), [wide] * 3 + spare, 16,
                              2 * 10**9, both, both_p, fwd, bwd, fs)
    up = lax.ppermute(up, "blk", toward)
    fwd, col = call(far_second_kernel, (stats, stats), [wide], 8, 10**9, second_o, fs, fwd, taps, bias)
    single = pltpu.VMEM((1, TILE, 2 * CH), jnp.bfloat16)
    bwd1, row1 = call(far_first0_kernel, (frame, frame), [single] * 2, 8, 5 * 10**8, first_o0, both, bwd)
    sent, flows, edge = call(functools.partial(far_first1_kernel, height),
                             (f32((FR, 24, W)), f32((FR, 8, W)), f32((FR, 4, W))),
                             [single, single, kept, kept] + spare[:2] + [narrow] + spare[2:], 12, 5 * 10**8,
                             both, both_p, second_o, first_o0, first_o1, bwd, fwd, col, bwd1, row1, part,
                             far=(1, 2))
    down = lax.ppermute(sent, "blk", back)
    edge_heavy = lax.ppermute(edge, "blk", [c for c in chip if early[c[0]]])
    rows, edge = call(functools.partial(flow_kernel, height), (f32((FR, 16, W)), f32((FR, 4, W))), [], 4, 10**6,
                      part, flows, sent, up, down)
    edge_light = lax.ppermute(edge, "blk", [c for c in chip if not early[c[0]]])
    return call(refine_kernel, f32((FR, 4, 2, W)), [], 4, 10**6, rows, edge_heavy, edge_light, taps, bias)


def solution(mesh):
    placed = (P("pair", "blk", None), P("pair", "blk", None), P(), P())
    return jax.shard_map(
        device_program,
        mesh=mesh,
        in_specs=placed,
        out_specs=P("pair", None, "blk", None),
        check_vma=False,
    )
```

```python
import functools
import math

import jax
import jax.numpy as jnp
import numpy as np
from jax import lax
from jax.experimental import pallas as pl
from jax.experimental.pallas import tpu as pltpu
from jax.sharding import PartitionSpec as P


W = 480
TILE = 960
CH = 128
FR = 2
MID = 240.0
SCALE = math.log2(math.e) / math.sqrt(CH)
LOW = 2.0**-60
HIGH = 2.0**100
NT = (((1,), (1,)), ((), ()))
NN = (((1,), (0,)), ((), ()))


def dot(a, b, dims):
    return lax.dot_general(a, b, dims, preferred_element_type=jnp.float32)


def takes(pos, size):
    upper = pos == size // 2
    return upper | ((pos % 2 == 1) & (pos != size // 2 - 1) & (pos != size - 1))


def side():
    pos, size = lax.axis_index("blk"), lax.axis_size("blk")
    even = pos % 2 == 0
    present = jnp.where(even, pos > 0, pos < size - 1)
    return even, takes(pos, size), present


def moments():
    lane = lax.broadcasted_iota(jnp.int32, (8, TILE), 1)
    row = lax.broadcasted_iota(jnp.int32, (8, TILE), 0)
    second = (lane >= W).astype(jnp.int32)
    col = lane - W * second - int(MID)
    value = jnp.where(row == 0, 1, jnp.where(row == 1, col, jnp.where(row == 2, second, 0)))
    return value.astype(jnp.float32).astype(jnp.bfloat16)


def split_into(dst, f, feat):
    scaled = feat.astype(jnp.float32) * SCALE
    hi = scaled.astype(jnp.bfloat16)
    dst[f, :, :CH] = hi
    dst[f, :, CH:] = (scaled - hi.astype(jnp.float32)).astype(jnp.bfloat16)


def twice_into(dst, f, feat):
    dst[f, :, :CH] = feat
    dst[f, :, CH:] = feat


def down_sums(weight):
    total = ramp = later = None
    for r in range(2):
        run = None
        for g in range(r * W, (r + 1) * W, 8):
            part = weight[g : g + 8]
            run = part if run is None else run + part
            ramp = run if ramp is None else ramp + run
        total = run if total is None else total + run
        later = run
    sub = lax.broadcasted_iota(jnp.int32, total.shape, 0).astype(jnp.float32)
    col = (W - MID + sub) * total - 8.0 * ramp
    rows = [jnp.sum(v, axis=0, keepdims=True) for v in (total, col, later)]
    return jnp.concatenate(rows + [jnp.zeros((5, total.shape[1]), jnp.float32)], axis=0)


def sums(lhs, rhs, f, down, mom=None):
    size = 256 if mom is None else 512
    cuts = [(n0, min(size, TILE - n0)) for n0 in range(0, TILE, size)]

    def scores(n0, w):
        return dot(lhs[f], rhs[f, n0 : n0 + w, :], NT)

    across = None
    ahead = scores(*cuts[0])
    for i, (n0, w) in enumerate(cuts):
        weight = jnp.exp2(ahead)
        if i + 1 < len(cuts):
            ahead = scores(*cuts[i + 1])
        down(n0, w, down_sums(weight))
        if mom is not None:
            part = dot(mom[:, n0 : n0 + w], weight.astype(jnp.bfloat16), NT)
            across = part if across is None else across + part
    return across


def merge(a, b):
    top = jnp.maximum(a[0], b[0])
    ka, kb = jnp.exp2(a[0] - top), jnp.exp2(b[0] - top)
    return (top,) + tuple(u * ka + v * kb for u, v in zip(a[1:], b[1:]))


def finish(total, mom_x, mom_y, row, height):
    col = lax.broadcasted_iota(jnp.int32, total.shape, 1).astype(jnp.float32) - MID
    return (mom_x / total - col) * (2.0 / W), (mom_y / total - row) * (2.0 / height)


def load_kernel(first, second, both, sems):
    pairs = [(first.at[f], both.at[0, f]) for f in range(FR)] + [(second.at[f], both.at[1, f]) for f in range(FR)]
    copies = [pltpu.make_async_copy(src, dst, sems.at[k]) for k, (src, dst) in enumerate(pairs)]
    for c in copies:
        c.start()
    for c in copies:
        c.wait()


def own_kernel(both, fwd, bwd, fs, ss):
    mom = moments()

    def frame(f, _):
        split_into(fs, f, both[0, f])
        twice_into(ss, f, both[1, f])

        def down(n0, w, part):
            fwd[f, :, n0 : n0 + w] = part

        bwd[f] = sums(ss, fs, f, down, mom)
        return 0

    lax.fori_loop(0, FR, frame, 0)


def shift_y(part, offset):
    row = lax.broadcasted_iota(jnp.int32, part.shape, 0)
    return part + jnp.where(row == 2, offset * part[0:1, :], 0.0)


def inside(x):
    return jnp.all((x[:, 0:1, :] >= LOW) & (x[:, 0:1, :] <= HIGH))


def exact(sources, feats, found, sems, jobs, tiles, near, far):
    index = lax.broadcasted_iota(jnp.int32, (TILE, 1), 0)
    second_row = (index >= W).astype(jnp.float32)
    column = index.astype(jnp.float32) - W * second_row - MID

    def frame(f, _):
        copies = [pltpu.make_async_copy(src.at[f], feats.at[k], sems.at[k]) for k, src in sources.items()]
        for c in copies:
            c.start()
        for c in copies:
            c.wait()

        def job(j, _):
            query = jnp.where(j == 0, 3, jnp.where(j == 1, 0, jnp.where(j == 2, 2, 5)))
            begin = jnp.where((j == 1) | (j == 2), 3, 0)
            end = begin + jnp.where(j < 2, tiles, 1)
            for n0 in range(0, TILE, CH):
                w = min(CH, TILE - n0)
                rows = feats[query, n0 : n0 + w, :]

                def step(k, old):
                    scores = dot(feats[k], rows, NT) * SCALE
                    rel = k - begin
                    offset = jnp.where(rel == 0, 0.0, jnp.where(rel == 1, near, far))
                    top = jnp.max(scores, axis=0, keepdims=True)
                    weight = jnp.exp2(scores - top)
                    total = jnp.sum(weight, axis=0, keepdims=True)
                    mom_x = jnp.sum(weight * column, axis=0, keepdims=True)
                    mom_y = jnp.sum(weight * second_row, axis=0, keepdims=True) + offset * total
                    return merge(old, (top, total, mom_x, mom_y))

                zero = jnp.zeros((1, w), jnp.float32)
                status = (jnp.full((1, w), -1e30, jnp.float32), zero, zero, zero)
                status = lax.fori_loop(begin, end, step, status)
                found[f, j, 0:4, n0 : n0 + w] = jnp.concatenate(status, axis=0)
            return 0

        lax.fori_loop(0, jobs, job, 0)
        return 0

    lax.fori_loop(0, FR, frame, 0)


def tiles_of(both, both_p):
    return {0: both.at[1], 1: both_p.at[1], 3: both.at[0], 4: both_p.at[0]}


def plain(part):
    return jnp.concatenate([jnp.zeros_like(part[0:1]), part[0:3]], axis=0)


def chip_kernel(both, both_p, fwd0, bwd0, fs, fwd, bwd, part, up, ss, fp, sp, feats, found, sems):
    even, heavy, _ = side()
    near = jnp.where(even, 2.0, -2.0)

    def frame(f, _):
        twice_into(ss, f, both[1, f])
        split_into(fp, f, both_p[0, f])
        twice_into(sp, f, both_p[1, f])

        def down_f(n0, w, part):
            fwd[f, :, n0 : n0 + w] = fwd0[f, :, n0 : n0 + w] + shift_y(part, near)

        def down_b(n0, w, part):
            bwd[f, :, n0 : n0 + w] = bwd0[f, :, n0 : n0 + w] + shift_y(part, near)

        sums(sp, fs, f, down_f)
        sums(fp, ss, f, down_b)
        return 0

    lax.fori_loop(0, FR, frame, 0)

    @pl.when(jnp.logical_not(heavy))
    def _():
        for f in range(FR):
            found[f, 0, 0:4, :] = plain(fwd[f])
            found[f, 1, 0:4, :] = plain(bwd[f])

        @pl.when(jnp.logical_not(inside(fwd) & inside(bwd)))
        def _():
            exact(tiles_of(both, both_p), feats, found, sems, 2, 2, near, near)

        for f in range(FR):
            for j in range(2):
                stat = found[f, j, 0:4, :]
                part[f, 4 * j : 4 * j + 4, :] = stat
                up[f, 4 * j : 4 * j + 4, :] = jnp.where(even, stat[:, :W], stat[:, W:])


def far_second_kernel(second_o, fs, fwd0, taps, bias, fwd, col, so):
    even, heavy, _ = side()
    far = jnp.where(even, -2.0, 2.0)

    @pl.when(heavy)
    def _():
        mom = moments()

        def frame(f, _):
            twice_into(so, f, second_o[f])

            def down(n0, w, part):
                fwd[f, :, n0 : n0 + w] = fwd0[f, :, n0 : n0 + w] + shift_y(part, far)

            col[f] = sums(so, fs, f, down, mom)
            return 0

        lax.fori_loop(0, FR, frame, 0)


def far_first_kernel(height, both, both_p, second_o, first_o, bwd0, fwd, col, part,
                     sent, flows, edge, fo, ss, bwd, row, feats, found, sems):
    even, heavy, present = side()
    far = jnp.where(even, -2.0, 2.0)

    @pl.when(jnp.logical_not(present))
    def _():
        for f in range(FR):
            pieces = []
            for j in range(2):
                stat = part[f, 4 * j : 4 * j + 4, :]
                stat = jnp.where(even, stat[:, W:], stat[:, :W])
                pieces.extend(finish(stat[1:2], stat[2:3], stat[3:4], jnp.where(even, 1.0, 0.0), height))
            edge[f] = jnp.concatenate(pieces, axis=0)

    @pl.when(heavy)
    def _():
        mom = moments()

        def frame(f, _):
            split_into(fo, f, first_o[f])
            twice_into(ss, f, both[1, f])

            def down(n0, w, part):
                bwd[f, :, n0 : n0 + w] = bwd0[f, :, n0 : n0 + w] + shift_y(part, far)

            row[f] = sums(fo, ss, f, down, mom)
            return 0

        lax.fori_loop(0, FR, frame, 0)
        for f in range(FR):
            for j, stat in enumerate((fwd, bwd, col, row)):
                found[f, j, 0:4, :] = plain(stat[f])

        @pl.when(jnp.logical_not(inside(fwd) & inside(bwd) & inside(col) & inside(row)))
        def _():
            sources = {**tiles_of(both, both_p), 2: second_o, 5: first_o}
            exact(sources, feats, found, sems, 4, 3, -far, far)

        for f in range(FR):
            maps = []
            for r in range(2):
                pieces = []
                for j in range(2):
                    stat = found[f, j, 0:4, :]
                    stat = stat[:, r * W : r * W + W]
                    pieces.extend(finish(stat[1:2], stat[2:3], stat[3:4], float(r), height))
                maps.append(jnp.concatenate(pieces, axis=0))
                flows[f, 4 * r : 4 * r + 4, :] = maps[r]
            edge[f] = jnp.where(even, maps[1], maps[0])
            sent[f, 16:20, :] = jnp.where(even, maps[0], maps[1])
            for j in range(2):
                stat = found[f, 2 + j, 0:4, :]
                sent[f, 8 * j : 8 * j + 4, :] = stat[:, :W]
                sent[f, 8 * j + 4 : 8 * j + 8, :] = stat[:, W:]
            sent[f, 20:24, :] = jnp.zeros((4, W), jnp.float32)


def flow_kernel(height, part, flows, sent, up, down, rows, edge):
    even, heavy, present = side()
    far = jnp.where(even, -2.0, 2.0)

    def stat(x, offset):
        return x[0:1], x[1:2], x[2:3], x[3:4] + offset * x[1:2]

    def place(f, halo):
        rows[f, 0:4, :] = jnp.where(even, halo, 0.0)
        rows[f, 12:16, :] = jnp.where(even, 0.0, halo)

    @pl.when(heavy)
    def _():
        for f in range(FR):
            halo = []
            for j in range(2):
                at = 8 * (1 - j)
                mine = jnp.where(even, sent[f, at + 4 : at + 8, :], sent[f, at : at + 4, :])
                _, total, mx, my = merge(stat(up[f, 4 * j : 4 * j + 4, :], 0.0), stat(mine, -far))
                halo.extend(finish(total, mx, my, jnp.where(even, 1.0, 0.0), height))
            place(f, jnp.concatenate(halo, axis=0))
            rows[f, 4:12, :] = flows[f]

    @pl.when(jnp.logical_not(heavy))
    def _():
        for f in range(FR):
            maps = []
            for r in range(2):
                pieces = []
                for j in range(2):
                    mine = part[f, 4 * j : 4 * j + 4, :]
                    at = 8 * (1 - j) + 4 * r
                    top, total, mx, my = stat(down[f, at : at + 4, :], far)
                    other = (jnp.where(present, top, -1e30), total, mx, my)
                    _, total, mx, my = merge(stat(mine[:, r * W : r * W + W], 0.0), other)
                    pieces.extend(finish(total, mx, my, float(r), height))
                maps.append(jnp.concatenate(pieces, axis=0))
                rows[f, 4 + 4 * r : 8 + 4 * r, :] = maps[r]
            edge[f] = jnp.where(even, maps[1], maps[0])
            place(f, jnp.where(present, down[f, 16:20, :], 0.0))


def refine_kernel(rows, edge_heavy, edge_light, taps, bias, out):
    even, _, _ = side()
    pos, size = lax.axis_index("blk"), lax.axis_size("blk")
    partner = jnp.where(even, pos + 1, pos - 1)
    from_heavy = takes(partner, size) | (partner == 0) | (partner == size - 1)
    none = jnp.zeros((16, 1), jnp.float32)
    for f in range(FR):
        mine = rows[f]
        other = jnp.where(from_heavy, edge_heavy[f], edge_light[f])
        full = jnp.concatenate(
            [jnp.where(even, mine[0:4], other), mine[4:12], jnp.where(even, other, mine[12:16])], axis=0
        )
        left = jnp.concatenate([none, full[:, : W - 1]], axis=1)
        right = jnp.concatenate([full[:, 1:], none], axis=1)
        patches = jnp.concatenate([left, full, right], axis=0)
        mixed = lax.dot_general(
            taps[...], patches, NN, precision=lax.Precision.HIGHEST, preferred_element_type=jnp.float32
        )
        mixed = mixed + bias[...] + full[4:12]
        for o in range(4):
            out[f, o, 0:1, :] = mixed[o : o + 1]
            out[f, o, 1:2, :] = mixed[4 + o : 5 + o]


def call(kernel, shapes, scratch, limit, flops, *args, hbm=(), far=()):
    spec = pl.BlockSpec(memory_space=pltpu.VMEM)
    anywhere = pl.BlockSpec(memory_space=pl.ANY)
    home = pl.BlockSpec(memory_space=pltpu.HBM)
    single = not isinstance(shapes, tuple)
    return pl.pallas_call(
        kernel,
        out_shape=shapes,
        in_specs=[home if i in hbm else anywhere if i in far else spec for i in range(len(args))],
        out_specs=spec if single else (spec,) * len(shapes),
        scratch_shapes=scratch,
        compiler_params=pltpu.CompilerParams(vmem_limit_bytes=limit << 20),
        cost_estimate=pl.CostEstimate(flops=flops, bytes_accessed=flops // 1000, transcendentals=0),
    )(*args)


def device_program(first, second, conv_weight, conv_bias):
    size = lax.axis_size("blk")
    height = 2 * size
    f32 = functools.partial(jax.ShapeDtypeStruct, dtype=jnp.float32)
    wide = pltpu.VMEM((FR, TILE, 2 * CH), jnp.bfloat16)
    kept = pltpu.VMEM((FR, 8, TILE), jnp.float32)
    spare = [pltpu.VMEM((6, TILE, CH), jnp.bfloat16), pltpu.VMEM((FR, 4, 8, TILE), jnp.float32)]
    spare.append(pltpu.SemaphoreType.DMA((6,)))
    chip = [(i, i ^ 1) for i in range(size)]
    heavy = [bool(takes(np.int32(i), size)) for i in range(size)]
    pairs = [(i, i + 1) for i in range(1, size - 1, 2)]
    toward = [(j, i) if heavy[i] else (i, j) for i, j in pairs]
    back = [(j, i) for i, j in toward]
    early = [heavy[i] or i in (0, size - 1) for i in range(size)]

    taps = conv_weight.transpose(0, 3, 2, 1)
    taps = jnp.stack([jnp.pad(taps, ((0, 0), (0, 0), (r, 1 - r), (0, 0))) for r in range(2)])
    taps = taps.reshape(8, 48)
    bias = jnp.concatenate([conv_bias, conv_bias]).reshape(8, 1)
    second_o = lax.ppermute(second, "blk", toward)
    first_o = lax.ppermute(first, "blk", toward)
    first, second = (pltpu.with_memory_space_constraint(x, pltpu.HBM) for x in (first, second))
    loaded = jax.ShapeDtypeStruct((2, FR, TILE, CH), jnp.bfloat16)
    both = call(load_kernel, loaded, [pltpu.SemaphoreType.DMA((4,))], 4, 10**6, first, second, hbm=(0, 1))
    both_p = lax.ppermute(both, "blk", chip)
    stats = f32((FR, 8, TILE))
    doubled = jax.ShapeDtypeStruct((FR, TILE, 2 * CH), jnp.bfloat16)
    own_out = (stats, stats, doubled)
    fwd, bwd, fs = call(own_kernel, own_out, [wide], 8, 10**9, both)
    fwd, bwd, part, up = call(chip_kernel, (stats, stats, stats, f32((FR, 8, W))), [wide] * 3 + spare, 16,
                              2 * 10**9, both, both_p, fwd, bwd, fs)
    up = lax.ppermute(up, "blk", toward)
    fwd, col = call(far_second_kernel, (stats, stats), [wide], 8, 10**9, second_o, fs, fwd, taps, bias)
    sent, flows, edge = call(functools.partial(far_first_kernel, height),
                             (f32((FR, 24, W)), f32((FR, 8, W)), f32((FR, 4, W))),
                             [wide, wide, kept, kept] + spare, 14, 10**9,
                             both, both_p, second_o, first_o, bwd, fwd, col, part, far=(1, 2))
    down = lax.ppermute(sent, "blk", back)
    edge_heavy = lax.ppermute(edge, "blk", [c for c in chip if early[c[0]]])
    rows, edge = call(functools.partial(flow_kernel, height), (f32((FR, 16, W)), f32((FR, 4, W))), [], 4, 10**6,
                      part, flows, sent, up, down)
    edge_light = lax.ppermute(edge, "blk", [c for c in chip if not early[c[0]]])
    return call(refine_kernel, f32((FR, 4, 2, W)), [], 4, 10**6, rows, edge_heavy, edge_light, taps, bias)


def solution(mesh):
    placed = (P("pair", "blk", None), P("pair", "blk", None), P(), P())
    return jax.shard_map(
        device_program,
        mesh=mesh,
        in_specs=placed,
        out_specs=P("pair", None, "blk", None),
        check_vma=False,
    )
```
